32 devices in a mesh: basin: 16 (over z, y, core), unit: 2 (over x).
Axes of the slice: x: 2, y: 2, z: 4, core: 2. Of those that a mesh axis runs over, the one named last changes fastest.
Arguments:
- forcing: bfloat16 [12, 32, 32768], P(None, None, ('basin', 'unit')), may hold values from -6 to 6
- hidden_init: bfloat16 [128, 32768], P(None, ('basin', 'unit')), may hold values from -0.8984375 to 0.8984375
- cell_init: float32 [128, 32768], P(None, ('basin', 'unit')), may hold values from -6 to 6
- w_input: bfloat16 [512, 32], replicated, may hold values from -1 to 1
- w_recur: bfloat16 [512, 128], replicated, may hold values from -0.5 to 0.5
- gate_bias: float32 [512], replicated, may hold values from -4 to 4
- w_head: float32 [128], replicated, may hold values from -0.5 to 0.5
- remap_dest: int32 [256, 8], P(('basin', 'unit')), may hold values from 0 to 15, all different within a row; in each aligned block of 8 rows (0 to 7, 8 to 15, ...) at most 8 rows name the same one
- remap_block: int32 [256, 8], P(('basin', 'unit')), may hold values from 0 to 7
- remap_weight: bfloat16 [256, 8, 128, 128], P(('basin', 'unit')), may hold values from -0.5 to 0.5
- route_kernel: float32 [256, 128, 128], P(('basin', 'unit'))
- carry_gain: float32 [256, 128], P(('basin', 'unit')), may hold values from 0.85 to 1
- block_count: int32 [16], replicated, may hold values from 1 to 16, as said below
- parent_section: int32 [16], replicated, may hold values from 1 to 16, as said below
- reservoir: int32 [16], replicated, may hold values 0 or 1
- release: float32 [12, 16], replicated, may hold values from 0.5 to 3
Outputs:
- discharge: float32 [12, 32768], P(None, ('basin', 'unit'))
The draws below stay inside these ranges and needn't reach their ends.
Inputs may be any that keep to these rules, and one draw needn't show every extreme that they name: `remap_dest`: in the rows of one device (aligned blocks of 8 rows) no value appears more than 8 times, and in some such block one value appears exactly 8 times; the 8 values of a row differ. `block_count`: the last section uses all 16 blocks. parent_section[s] > s for every section; the last section's value is 16 (the outlet), every other value is below 16. A section s below 8 flows into s + 8 or the section after it; every other section flows into one of the next two.
All inputs are finite; a program needn't handle non-finite values.
Results may differ from the reference program's by a relative error of at most 0.017.
Values may be sent and summed in bfloat16 or wider, within the bound.
No kernel may reach another device: no remote copies, remote signals or barrier semaphores. Data moves between devices by JAX's collectives and lax.ppermute only.
A program may use at most 64 MiB of HBM per device.

```python
import math
import jax
import jax.numpy as jnp
import numpy as np
from jax import lax

STATE = 128
FEATURES = 32
STEPS = 12
BLOCK = 128
TOP = 8
UNITS_DEV = 1024
RBLOCKS_DEV = 8
UNIT_BLOCKS_DEV = 8
UNITS = 32768
UNIT_BLOCKS = 256
SECTIONS = 16
SEC_BLOCKS = 16
REACH_BLOCKS = 256
REACHES = 32768
MOST = 8
N_BASIN = 16
N_UNIT = 2


def draw_route_kernel(key, part):
    key_diag, key_lower = jax.random.split(key)
    kernel_shape = (REACH_BLOCKS, BLOCK, BLOCK)
    row_index = lax.broadcasted_iota(jnp.int32, kernel_shape, 1)
    col_index = lax.broadcasted_iota(jnp.int32, kernel_shape, 2)
    diagonal = jax.random.uniform(key_diag, kernel_shape, jnp.float32, 0.5, 1.0)
    lower_part = jax.random.uniform(key_lower, kernel_shape, jnp.float32, -0.9, 0.9)
    scaled = lower_part / jnp.sqrt(row_index.astype(jnp.float32) + 1.0)
    return jnp.where(row_index == col_index, diagonal, jnp.where(col_index < row_index, scaled, 0.0))


def draw_block_count(key, part):
    counts_drawn = jax.random.randint(key, (SECTIONS,), 1, SEC_BLOCKS + 1, dtype=jnp.int32)
    return counts_drawn.at[SECTIONS - 1].set(SEC_BLOCKS)


def draw_parent_section(key, part):
    position = jnp.arange(SECTIONS, dtype=jnp.int32)
    half_count = SECTIONS // 2
    trib_low = position + half_count
    trib_high = jnp.minimum(position + half_count + 2, SECTIONS)
    main_low = position + 1
    main_high = jnp.maximum(jnp.minimum(position + 3, SECTIONS), position + 2)
    lower_end = jnp.where(position < half_count, trib_low, main_low)
    upper_end = jnp.where(position < half_count, trib_high, main_high)
    return jax.random.randint(key, (SECTIONS,), lower_end, upper_end, dtype=jnp.int32)


def place_ends(entries, stream_key, smallest, high):
    extent = entries.shape
    index_at = [jax.random.randint(jax.random.fold_in(stream_key, axis), (), 0, extent[axis]) for axis in range(len(extent))]
    entries = entries.at[tuple(index_at)].set(smallest)
    longest = extent.index(max(extent))
    index_at[longest] = (index_at[longest] + 1) % extent[longest]
    return entries.at[tuple(index_at)].set(high)


def shard_levels(key, dims, cuts, smallest, largest):
    gain, own = 1.0, jax.random.fold_in(key, 6)
    for dim, shards_of in cuts:
        draws = jnp.exp(jax.random.uniform(jax.random.fold_in(own, dim), (shards_of,), jnp.float32, smallest / len(cuts), largest / len(cuts)))
        gain = gain * jnp.repeat(draws, dims[dim] // shards_of).reshape([-1 if axis == dim else 1 for axis in range(len(dims))])
    return gain


def assign_block(stream_key, own, number, rows, number_of, top, bound, skew):
    order = jax.random.permutation(stream_key, number_of)
    heavy_load, common = shares(number_of, rows * top, bound, skew, True), shares(number_of, rows * top, bound, skew, False)
    places = jnp.arange(number_of)

    def named(tallies, rotation):
        used = int((tallies > 0).sum())
        fixed = max(1, used // 4)
        shifted = fixed + (places - fixed + rotation * (used - fixed)) % max(1, number_of - fixed)
        return jnp.zeros((number_of,), jnp.int32).at[order[jnp.where(places < fixed, places, shifted)]].set(jnp.asarray(tallies, jnp.int32))

    tallies = jnp.where(number % 4 == 0, named(heavy_load, number // 4), named(common, number - number // 4 - 1))
    mixed = jax.random.permutation(jax.random.fold_in(own, 3), number_of)
    giver, sink = mixed[0:number_of // 2 * 2:2], mixed[1:number_of // 2 * 2:2]
    room = jnp.minimum(tallies[giver] - 1, bound - tallies[sink]) // 2
    room = jnp.where((giver == order[0]) | (sink == order[0]) | (tallies[sink] == 0), 0, jnp.maximum(room, 0))
    shifted = jax.random.randint(jax.random.fold_in(own, 4), (number_of // 2,), 0, 1 << 20) % (room + 1)
    tallies = tallies.at[giver].add(-shifted).at[sink].add(shifted)
    members = jnp.searchsorted(jnp.cumsum(tallies), jnp.arange(rows * top), side="right").astype(jnp.int32)
    grid = members.reshape(top, rows).T
    grid = grid[jax.random.permutation(jax.random.fold_in(own, 1), rows)]
    rotation = jax.random.randint(jax.random.fold_in(own, 2), (rows, 1), 0, top)
    return jnp.take_along_axis(grid, (jnp.arange(top)[None, :] + rotation) % top, axis=1)


def shares(amount, total, most, skew, full):
    loads = [(1 << 20) // math.isqrt(standing ** skew) + 1 for standing in range(1, amount + 1)]
    largest = most if full else min(most, max(-(-total // amount), total * loads[0] // sum(loads)))
    least = 1 if total - largest >= amount - 1 else 0
    holding, rest = [largest] + [least] * (amount - 1), total - largest - least * (amount - 1)
    while rest > 0:
        candidates = [i for i in range(1, amount) if holding[i] < largest] or [i for i in range(1, amount) if holding[i] < most]
        pool, budget = sum([loads[i] for i in candidates]), rest
        for i in candidates:
            extra = min(most - holding[i], max(1, budget * loads[i] // pool), rest)
            holding[i] = holding[i] + extra
            rest = rest - extra
    return np.array(holding)


def bell_draw(rng, shape, scale, reach, cuts=(), kind=jnp.bfloat16):
    result = jax.random.normal(rng, shape, jnp.float32) * scale
    if len(cuts) > 0:
        result = shard_levels(rng, shape, cuts, -0.22, 0.18) * result
    return jnp.clip(result, min=-reach, max=reach).astype(kind)


def setup_inputs(seed: int = 0) -> dict:
    key_list = jax.random.split(jax.random.key(seed), 17)
    forcing = bell_draw(key_list[0], (STEPS, FEATURES, UNITS), 1.0, 6.0, ((2, 32),))
    hidden_init = jnp.clip(jax.random.uniform(key_list[1], (STATE, UNITS), jnp.float32, -0.8984375, 0.8984375) * shard_levels(key_list[1], (STATE, UNITS), ((1, 32),), -0.4, 0.0), -0.8984375, 0.8984375).astype(jnp.bfloat16)
    cell_init = bell_draw(key_list[2], (STATE, UNITS), 1.0, 6.0, ((1, 32),), jnp.float32)
    w_input = bell_draw(key_list[3], (4 * STATE, FEATURES), FEATURES ** -0.5, 1.0)
    w_recur = bell_draw(key_list[4], (4 * STATE, STATE), STATE ** -0.5, 0.5)
    gate_bias = bell_draw(key_list[5], (4 * STATE,), 1.0, 4.0, (), jnp.float32)
    w_head = bell_draw(key_list[6], (STATE,), STATE ** -0.5, 0.5, (), jnp.float32)
    remap_dest_keys = jax.random.split(jax.random.fold_in(key_list[7], 1), UNIT_BLOCKS // UNIT_BLOCKS_DEV)
    remap_dest_turns = jax.random.permutation(jax.random.fold_in(key_list[7], 3), UNIT_BLOCKS // UNIT_BLOCKS_DEV)
    remap_dest = jax.vmap(lambda own, number: assign_block(jax.random.fold_in(key_list[7], 2), own, number, UNIT_BLOCKS_DEV, N_BASIN, TOP, MOST, 2))(remap_dest_keys, remap_dest_turns).reshape((UNIT_BLOCKS, TOP))
    remap_block = place_ends(jax.random.randint(key_list[8], (UNIT_BLOCKS, TOP), 0, RBLOCKS_DEV), jax.random.fold_in(key_list[8], 1), 0, RBLOCKS_DEV - 1).astype(jnp.int32)
    remap_weight = bell_draw(key_list[9], (UNIT_BLOCKS, TOP, BLOCK, BLOCK), BLOCK ** -0.5, 0.5, ((0, 32),))
    route_kernel = draw_route_kernel(jax.random.fold_in(key_list[16], 71), 0)
    carry_gain = jnp.clip(0.85 + 0.14999998 * jax.random.uniform(key_list[11], (REACH_BLOCKS, BLOCK), jnp.float32) ** shard_levels(key_list[11], (REACH_BLOCKS, BLOCK), ((0, 32),), -0.2, 0.2), 0.85, 1.0)
    block_count = draw_block_count(jax.random.fold_in(key_list[16], 71), 0)
    parent_section = draw_parent_section(jax.random.fold_in(key_list[16], 71), 0)
    reservoir = place_ends((jax.random.randint(key_list[14], (SECTIONS,), 0, 4) < 1).astype(jnp.int32), jax.random.fold_in(key_list[14], 1), 0, 1)
    release = jnp.clip(jax.random.uniform(key_list[15], (STEPS, SECTIONS), jnp.float32, 0.5, 3.0), 0.5, 3.0)
    return dict(forcing=forcing, hidden_init=hidden_init, cell_init=cell_init, w_input=w_input, w_recur=w_recur, gate_bias=gate_bias, w_head=w_head, remap_dest=remap_dest, remap_block=remap_block, remap_weight=remap_weight, route_kernel=route_kernel, carry_gain=carry_gain, block_count=block_count, parent_section=parent_section, reservoir=reservoir, release=release)


PRECISE = lax.Precision.HIGHEST


def lstm_runoff(forcing_one, hidden_one, cell_one, w_input, w_recur, gate_bias, w_head):
    def lstm_step(state_pair, frame_now):
        hidden, cell_state = state_pair
        gate_sum = jnp.dot(w_input, frame_now, preferred_element_type=jnp.float32)
        gate_sum = gate_sum + jnp.dot(w_recur, hidden, preferred_element_type=jnp.float32) + gate_bias[:, None]
        in_gate = jax.nn.sigmoid(gate_sum[0:STATE])
        forget = jax.nn.sigmoid(gate_sum[STATE:2 * STATE])
        cand_gate = jnp.tanh(gate_sum[2 * STATE:3 * STATE])
        out_gate = jax.nn.sigmoid(gate_sum[3 * STATE:])
        cell_state = forget * cell_state + in_gate * cand_gate
        hidden = (out_gate * jnp.tanh(cell_state)).astype(jnp.bfloat16)
        runoff = jax.nn.softplus(jnp.sum(w_head[:, None] * hidden.astype(jnp.float32), axis=0)).astype(jnp.bfloat16)
        return (hidden, cell_state), runoff

    final_pair, runoff = lax.scan(lstm_step, (hidden_one, cell_one), forcing_one)
    return runoff


def reference(forcing, hidden_init, cell_init, w_input, w_recur, gate_bias, w_head, remap_dest, remap_block, remap_weight, route_kernel, carry_gain, block_count, parent_section, reservoir, release):
    device_total = N_BASIN * N_UNIT
    forcing_dev = forcing.reshape(STEPS, FEATURES, device_total, UNITS_DEV).transpose(2, 0, 1, 3)
    hidden_dev = hidden_init.reshape(STATE, device_total, UNITS_DEV).transpose(1, 0, 2)
    cell_dev = cell_init.reshape(STATE, device_total, UNITS_DEV).transpose(1, 0, 2)
    dest_dev = remap_dest.reshape(device_total, UNIT_BLOCKS_DEV, TOP)
    block_dev = remap_block.reshape(device_total, UNIT_BLOCKS_DEV, TOP)
    weight_dev = remap_weight.reshape(device_total, UNIT_BLOCKS_DEV, TOP, BLOCK, BLOCK)

    def remap_device(lateral, inputs):
        device_id, forcing_one, hidden_one, cell_one, dest_one, block_one, weight_one = inputs
        runoff = lstm_runoff(forcing_one, hidden_one, cell_one, w_input, w_recur, gate_bias, w_head)
        blocks = runoff.reshape(STEPS, UNIT_BLOCKS_DEV, BLOCK).astype(jnp.float32)
        contrib = jnp.einsum("sub,ukbr->uksr", blocks, weight_one.astype(jnp.float32))
        contrib = lax.optimization_barrier(contrib.astype(jnp.bfloat16)).astype(jnp.float32)
        target = (dest_one * N_UNIT + device_id % N_UNIT) * RBLOCKS_DEV + block_one
        lateral = lateral.at[target.reshape(-1)].add(contrib.reshape(UNIT_BLOCKS_DEV * TOP, STEPS, BLOCK))
        return lateral, None

    lateral_init = jnp.zeros((REACH_BLOCKS, STEPS, BLOCK), jnp.float32)
    lateral, unused = lax.scan(remap_device, lateral_init, (jnp.arange(device_total, dtype=jnp.int32), forcing_dev, hidden_dev, cell_dev, dest_dev, block_dev, weight_dev))

    lateral_sec = lateral.reshape(SECTIONS, SEC_BLOCKS, STEPS, BLOCK)
    kernel_sec = route_kernel.reshape(SECTIONS, SEC_BLOCKS, BLOCK, BLOCK)
    gain_sec = carry_gain.reshape(SECTIONS, SEC_BLOCKS, BLOCK)

    def route_section(inflow_acc, inputs):
        section, lateral_one, kernel_one, gain_one, count_one, dam_flag, parent_one, release_one = inputs

        def route_block(carry_in, block_inputs):
            position, lateral_blk, kernel_blk, gain_blk = block_inputs
            flow_blk = jnp.dot(lateral_blk, kernel_blk.T, precision=PRECISE) + carry_in[:, None] * gain_blk[None, :]
            in_use = position < count_one
            flow_blk = jnp.where(in_use, flow_blk, 0.0)
            carry_out = jnp.where(in_use, flow_blk[:, BLOCK - 1], carry_in)
            return carry_out, flow_blk

        outflow, flow_all = lax.scan(route_block, inflow_acc[section], (jnp.arange(SEC_BLOCKS, dtype=jnp.int32), lateral_one, kernel_one, gain_one))
        passed = jnp.where(dam_flag == 1, release_one, outflow)
        inflow_acc = inflow_acc.at[parent_one].add(passed)
        return inflow_acc, flow_all

    acc_init = jnp.zeros((SECTIONS + 1, STEPS), jnp.float32)
    final_acc, flow_all = lax.scan(route_section, acc_init, (jnp.arange(SECTIONS, dtype=jnp.int32), lateral_sec, kernel_sec, gain_sec, block_count, reservoir, parent_section, release.T))
    return flow_all.transpose(2, 0, 1, 3).reshape(STEPS, REACHES)
```

```python
import functools

import jax
import jax.numpy as jnp
from jax import lax
from jax.experimental import pallas as pl
from jax.experimental.pallas import tpu as pltpu
from jax.sharding import PartitionSpec as P

PRECISE = lax.Precision.HIGHEST
AXES = ("basin", "unit")
ROW_PAD = 16


def stage_bits(size):
    return [bit for bit in range(size.bit_length() - 1)]


def slot_of(relative, size):
    slot = relative * 0
    for bit in stage_bits(size):
        slot = slot * 2 + ((relative >> bit) & 1)
    return slot


def split3(x):
    high = x.astype(jnp.bfloat16)
    rest = x - high.astype(jnp.float32)
    middle = rest.astype(jnp.bfloat16)
    low = (rest - middle.astype(jnp.float32)).astype(jnp.bfloat16)
    return high, middle, low


def units_kernel(
    dest_ref,
    block_ref,
    forcing_ref,
    hidden_ref,
    cell_ref,
    w_input_ref,
    w_recur_ref,
    bias_ref,
    head_ref,
    weight_hbm,
    keep_ref,
    send_ref,
    table,
    hidden,
    cell,
    head_sum,
    weight,
    slots,
    packed,
    sem,
    *,
    size,
    reach_blocks,
    chunk,
):
    steps, features, units = forcing_ref.shape
    state = hidden_ref.shape[0]
    unit_blocks, fan_out, block, _ = weight_hbm.shape
    gates = 4 * state
    depth = state + features + ROW_PAD
    fetch = pltpu.make_async_copy(weight_hbm, weight, sem)
    fetch.start()

    for gate in range(4):
        rows = pl.ds(gate * state, state)
        scale = 0.5 if gate == 2 else 0.25
        table[rows, 0:state] = (w_recur_ref[rows, :].astype(jnp.float32) * scale).astype(jnp.bfloat16)
    row = lax.broadcasted_iota(jnp.int32, (state - features, gates), 0)
    parts = [part.astype(jnp.float32) for part in split3(bias_ref[...])]
    bias_rows = jnp.zeros((state - features, gates), jnp.float32)
    for at, part in enumerate(parts):
        bias_rows = jnp.where(row == at, jnp.broadcast_to(part, bias_rows.shape), bias_rows)
    tail = jnp.concatenate([w_input_ref[...].astype(jnp.float32), bias_rows], axis=0)
    lane = lax.broadcasted_iota(jnp.int32, tail.shape, 1)
    tail = jnp.where((lane >= 2 * state) & (lane < 3 * state), tail, tail * 0.5)
    for gate in range(4):
        piece = tail[:, gate * state : (gate + 1) * state]
        table[gate * state : (gate + 1) * state, state : 2 * state] = piece.T.astype(jnp.bfloat16)
    row = lax.broadcasted_iota(jnp.int32, (ROW_PAD, state), 0)
    head_rows = jnp.zeros((ROW_PAD, state), jnp.float32)
    for at, part in enumerate(split3(head_ref[...] * 0.5)):
        head_rows = jnp.where(
            row == at, jnp.broadcast_to(part.astype(jnp.float32), head_rows.shape), head_rows
        )
    table[gates : gates + ROW_PAD, 0:state] = head_rows.astype(jnp.bfloat16)
    table[gates : gates + ROW_PAD, state : 2 * state] = jnp.zeros((ROW_PAD, state), jnp.bfloat16)
    hidden[...] = hidden_ref[...] + hidden_ref[...]
    cell[...] = cell_ref[...]
    head_sum[...] = jnp.zeros_like(head_sum)
    slots[...] = jnp.zeros_like(slots)
    ones = jnp.ones((ROW_PAD, chunk), jnp.bfloat16)

    def step(now, carry):
        for first in range(0, units, chunk):
            cols = pl.ds(first, chunk)
            operand = jnp.concatenate([hidden[:, cols], forcing_ref[now, :, cols], ones], axis=0)
            total = jnp.dot(table[:, 0:depth], operand, preferred_element_type=jnp.float32)
            head_sum[pl.ds((now + ROW_PAD - 1) % ROW_PAD, 1), cols] = (
                total[gates : gates + 1] + total[gates + 1 : gates + 2] + total[gates + 2 : gates + 3]
            )
            in_gate = jnp.tanh(total[0:state]) + 1.0
            forget = jnp.tanh(total[state : 2 * state]) + 1.0
            candidate = jnp.tanh(total[2 * state : 3 * state])
            out_gate = jnp.tanh(total[3 * state : 4 * state]) + 1.0
            after = (forget * cell[:, cols] + in_gate * candidate) * 0.5
            cell[:, cols] = after
            hidden[:, cols] = (out_gate * jnp.tanh(after)).astype(jnp.bfloat16)
        return carry

    lax.fori_loop(0, steps, step, 0)
    last = jnp.dot(
        table[gates : gates + ROW_PAD, 0:state], hidden[...], preferred_element_type=jnp.float32
    )
    head_sum[steps - 1 : steps, :] = last[0:1] + last[1:2] + last[2:3]
    runoff = jax.nn.softplus(head_sum[...]).astype(jnp.bfloat16)

    me = lax.axis_index("basin")
    fetch.wait()
    for group in range(unit_blocks):
        left = runoff[:, group * block : (group + 1) * block]
        for k in range(fan_out):
            contrib = jnp.dot(left, weight[group, k], preferred_element_type=jnp.float32)
            slot = slot_of(dest_ref[group, k] ^ me, size) * reach_blocks + block_ref[group, k]
            slots[slot] = slots[slot] + contrib
    half = size // 2

    def pack(at):
        for blk in range(reach_blocks):
            packed[at, blk * steps : (blk + 1) * steps, :] = slots[at * reach_blocks + blk, 0:steps, :]

    if size <= 16:
        for at in range(size):
            pack(at)
    else:

        def pack_step(at, carry):
            pack(at)
            return carry

        lax.fori_loop(0, size, pack_step, 0)
    keep_ref[...] = packed[0:half].astype(jnp.bfloat16)
    send_ref[...] = packed[half:size].astype(jnp.bfloat16)


def units_call(forcing, hidden_init, cell_init, w_input, w_recur, gate_bias, w_head, dest, blk, weight, reach_blocks):
    size = lax.axis_size("basin")
    steps, features, units = forcing.shape
    state = hidden_init.shape[0]
    gates = 4 * state
    block = weight.shape[3]
    chunk = 256
    half = jax.ShapeDtypeStruct((size // 2, reach_blocks * steps, block), jnp.bfloat16)
    vmem = pl.BlockSpec(memory_space=pltpu.VMEM)
    smem = pl.BlockSpec(memory_space=pltpu.SMEM)
    return pl.pallas_call(
        functools.partial(units_kernel, size=size, reach_blocks=reach_blocks, chunk=chunk),
        out_shape=(half, half),
        in_specs=[smem, smem] + [vmem] * 7 + [pl.BlockSpec(memory_space=pl.ANY)],
        out_specs=(vmem, vmem),
        scratch_shapes=[
            pltpu.VMEM((gates + ROW_PAD, 2 * state), jnp.bfloat16),
            pltpu.VMEM((state, units), jnp.bfloat16),
            pltpu.VMEM((state, units), jnp.float32),
            pltpu.VMEM((ROW_PAD, units), jnp.float32),
            pltpu.VMEM(weight.shape, weight.dtype),
            pltpu.VMEM((size * reach_blocks, ROW_PAD, block), jnp.float32),
            pltpu.VMEM((size, reach_blocks * steps, block), jnp.float32),
            pltpu.SemaphoreType.DMA,
        ],
        compiler_params=pltpu.CompilerParams(vmem_limit_bytes=(16 << 20) + size * (192 << 10)),
        name="units",
    )(
        dest,
        blk,
        forcing,
        hidden_init,
        cell_init,
        w_input.T,
        w_recur,
        gate_bias.reshape(1, gates),
        w_head.reshape(1, state),
        weight,
    )


def route_kernel_body(
    count_ref, mine_ref, other_ref, kernel_ref, gain_ref, flow_ref, map_ref, *, steps, copies
):
    reach_blocks, block, _ = kernel_ref.shape
    lateral = mine_ref[...].astype(jnp.float32) + other_ref[...].astype(jnp.float32)
    first = lax.axis_index("unit") * reach_blocks
    count = count_ref[lax.axis_index("basin")]
    shift = jnp.zeros((steps, block), jnp.float32)
    factor = jnp.ones((1, block), jnp.float32)
    for blk in range(reach_blocks):
        rows = slice(blk * steps, (blk + 1) * steps)
        flow = lax.dot_general(
            lateral[rows], kernel_ref[blk], (((1,), (1,)), ((), ())), precision=PRECISE,
            preferred_element_type=jnp.float32,
        )
        flow_ref[rows, :] = flow
        gain = gain_ref[blk : blk + 1, :]
        live = first + blk < count
        shift = jnp.where(live, flow + shift * gain, shift)
        factor = jnp.where(live, factor * gain, factor)
    tile = jnp.concatenate(
        [
            jnp.broadcast_to(shift[:, block - 1 : block], (steps, block)),
            jnp.broadcast_to(factor[:, block - 1 : block], (ROW_PAD - steps, block)),
        ],
        axis=0,
    )
    for at in range(copies):
        map_ref[at] = tile


def finish_kernel(
    count_ref, parent_ref, reservoir_ref, release_ref, map_ref, flow_ref, gain_ref, out_ref, inflow, *, steps
):
    reach_blocks, block = gain_ref.shape
    size, unit_size = lax.axis_size("basin"), lax.axis_size("unit")
    basin, unit = lax.axis_index("basin"), lax.axis_index("unit")
    inflow[...] = jnp.zeros_like(inflow)

    def join(section, head):
        for at in range(unit_size):
            tile = map_ref[section * unit_size + at]
            head = tile + jnp.broadcast_to(tile[steps : steps + 1], tile.shape) * head
        return head

    def tree(section, carry):
        outflow = join(section, inflow[section])
        given = jnp.broadcast_to(release_ref[section], outflow.shape)
        passed = jnp.where(reservoir_ref[section] == 1, given, outflow)
        parent = parent_ref[section]
        inflow[parent] = inflow[parent] + passed
        return carry

    lax.fori_loop(0, size, tree, 0)
    head = inflow[basin]
    for at in range(unit_size - 1):
        tile = map_ref[basin * unit_size + at]
        through = tile + jnp.broadcast_to(tile[steps : steps + 1], tile.shape) * head
        head = jnp.where(at < unit, through, head)
    carry = head[0:steps]
    count = count_ref[basin]
    for blk in range(reach_blocks):
        live = unit * reach_blocks + blk < count
        flow = flow_ref[blk * steps : (blk + 1) * steps, :] + carry * gain_ref[blk : blk + 1, :]
        out_ref[:, blk * block : (blk + 1) * block] = jnp.where(live, flow, 0.0)
        carry = jnp.where(live, jnp.broadcast_to(flow[:, block - 1 : block], carry.shape), carry)


def shards(
    forcing,
    hidden_init,
    cell_init,
    w_input,
    w_recur,
    gate_bias,
    w_head,
    remap_dest,
    remap_block,
    remap_weight,
    route_kernel,
    carry_gain,
    block_count,
    parent_section,
    reservoir,
    release,
):
    steps = forcing.shape[0]
    reach_blocks, block, _ = route_kernel.shape
    size, unit_size = lax.axis_size("basin"), lax.axis_size("unit")
    keep, send = units_call(
        forcing, hidden_init, cell_init, w_input, w_recur, gate_bias, w_head,
        remap_dest, remap_block, remap_weight, reach_blocks,
    )
    for at, bit in enumerate(stage_bits(size)):
        if at > 0:
            total = (keep.astype(jnp.float32) + got.astype(jnp.float32)).astype(jnp.bfloat16)
            half = total.shape[0] // 2
            keep, send = total[:half], total[half:]
        got = lax.ppermute(send, "basin", [(i, i ^ (1 << bit)) for i in range(size)])
    vmem = pl.BlockSpec(memory_space=pltpu.VMEM)
    smem = pl.BlockSpec(memory_space=pltpu.SMEM)
    copies = size * unit_size
    flow, own = pl.pallas_call(
        functools.partial(route_kernel_body, steps=steps, copies=copies),
        out_shape=(
            jax.ShapeDtypeStruct((reach_blocks * steps, block), jnp.float32),
            jax.ShapeDtypeStruct((copies, ROW_PAD, block), jnp.float32),
        ),
        in_specs=[smem] + [vmem] * 4,
        out_specs=(vmem, vmem),
        name="route",
    )(block_count, keep[0], got[0], route_kernel, carry_gain)
    maps = lax.all_to_all(own, AXES, split_axis=0, concat_axis=0, tiled=True)
    given = jnp.pad(release.T, ((0, 0), (0, ROW_PAD - steps)))[:, :, None]
    return pl.pallas_call(
        functools.partial(finish_kernel, steps=steps),
        out_shape=jax.ShapeDtypeStruct((steps, reach_blocks * block), jnp.float32),
        in_specs=[smem, smem, smem] + [vmem] * 4,
        out_specs=vmem,
        scratch_shapes=[pltpu.VMEM((size + 1, ROW_PAD, block), jnp.float32)],
        name="finish",
    )(block_count, parent_section, reservoir, given, maps, flow, carry_gain)


def solution(mesh):
    placed = (
        P(None, None, AXES),
        P(None, AXES),
        P(None, AXES),
        P(),
        P(),
        P(),
        P(),
        P(AXES, None),
        P(AXES, None),
        P(AXES, None, None, None),
        P(AXES, None, None),
        P(AXES, None),
        P(),
        P(),
        P(),
        P(),
    )
    return jax.shard_map(
        shards, mesh=mesh, in_specs=placed, out_specs=P(None, AXES), check_vma=False
    )
```

```python
import functools

import jax
import jax.numpy as jnp
from jax import lax
from jax.experimental import pallas as pl
from jax.experimental.pallas import tpu as pltpu
from jax.sharding import PartitionSpec as P

PRECISE = lax.Precision.HIGHEST
AXES = ("basin", "unit")
PAD = 16
VMEM = pl.BlockSpec(memory_space=pltpu.VMEM)
SMEM = pl.BlockSpec(memory_space=pltpu.SMEM)
HBM = pl.BlockSpec(memory_space=pltpu.HBM)


def in_hbm(*arrays):
    return [pltpu.with_memory_space_constraint(x, pltpu.HBM) for x in arrays]


def in_vmem(*arrays):
    return [pltpu.with_memory_space_constraint(x, pltpu.VMEM) for x in arrays]


def stage_bits(size):
    return range(size.bit_length() - 1)


def slot_of(relative, size):
    slot = relative * 0
    for bit in stage_bits(size):
        slot = slot * 2 + ((relative >> bit) & 1)
    return slot


def split3(x):
    high = x.astype(jnp.bfloat16)
    rest = x - high.astype(jnp.float32)
    middle = rest.astype(jnp.bfloat16)
    low = (rest - middle.astype(jnp.float32)).astype(jnp.bfloat16)
    return high, middle, low


def repeat(count, body):
    if count <= 16:
        for at in range(count):
            body(at)
    else:
        lax.fori_loop(0, count, lambda at, carry: (body(at), carry)[1], 0)


def prep_kernel(count_hbm, route_hbm, gain_hbm, share_ref, last_ref, gain_ref, count_ref, sems, *, size):
    reach_blocks, block = gain_hbm.shape
    copies = [
        pltpu.make_async_copy(route_hbm.at[:, block - 1, :], last_ref, sems.at[0]),
        pltpu.make_async_copy(gain_hbm, gain_ref, sems.at[1]),
        pltpu.make_async_copy(count_hbm, count_ref, sems.at[2]),
    ]
    for copy in copies:
        copy.start()
    for copy in copies:
        copy.wait()
    first = lax.axis_index("unit") * reach_blocks
    count = count_ref[lax.axis_index("basin")]
    factor = jnp.ones((1, block), jnp.float32)
    rows = [None] * reach_blocks
    for blk in reversed(range(reach_blocks)):
        live = first + blk < count
        rows[blk] = jnp.where(live, factor * last_ref[blk : blk + 1, :], 0.0)
        ratio = jnp.broadcast_to(gain_ref[blk : blk + 1, block - 1 : block], (1, block))
        factor = jnp.where(live, factor * ratio, factor)
    rows.append(factor * (1.0 / size))
    rows.append(jnp.zeros((PAD - len(rows), block), jnp.float32))
    tile = jnp.concatenate(rows, axis=0)

    def spread(at):
        share_ref[at] = tile

    repeat(size, spread)


def lstm_kernel(
    w_recur_hbm,
    w_input_hbm,
    bias_hbm,
    head_hbm,
    hidden_hbm,
    cell_hbm,
    release_hbm,
    forcing_hbm,
    weight_hbm,
    route_hbm,
    gain_hbm,
    runoff_ref,
    weight_ref,
    route_ref,
    gain_ref,
    given_ref,
    w_recur_ref,
    w_input_ref,
    bias_ref,
    head_ref,
    hidden,
    cell,
    release_ref,
    forcing_ref,
    table,
    head_sum,
    square,
    frame_sems,
    sems,
    *,
    chunk,
):
    steps, features, units = forcing_hbm.shape
    state = hidden_hbm.shape[0]
    gates = 4 * state
    depth = state + features + PAD
    pairs = [
        (w_recur_hbm, w_recur_ref),
        (w_input_hbm, w_input_ref),
        (bias_hbm, bias_ref),
        (head_hbm, head_ref),
        (hidden_hbm, hidden),
        (cell_hbm, cell),
        (release_hbm, release_ref),
        (gain_hbm, gain_ref),
        (weight_hbm, weight_ref),
        (route_hbm, route_ref),
    ]
    copies = [pltpu.make_async_copy(a, b, sems.at[at]) for at, (a, b) in enumerate(pairs)]

    def frame(now):
        return pltpu.make_async_copy(forcing_hbm.at[now], forcing_ref.at[now], frame_sems.at[now])

    for copy in copies[:7]:
        copy.start()
    for now in range(steps):
        frame(now).start()
    for copy in copies[7:]:
        copy.start()
    square[...] = jnp.zeros_like(square)
    table[gates : gates + PAD, state : 2 * state] = jnp.zeros((PAD, state), jnp.bfloat16)
    head_sum[...] = jnp.zeros_like(head_sum)
    copies[0].wait()
    for gate in range(4):
        at = pl.ds(gate * state, state)
        scale = 0.5 if gate == 2 else 0.25
        table[at, 0:state] = (w_recur_ref[at, :].astype(jnp.float32) * scale).astype(jnp.bfloat16)
    for copy in copies[1:4]:
        copy.wait()
    row = lax.broadcasted_iota(jnp.int32, (state - features, gates), 0)
    bias_rows = jnp.zeros((state - features, gates), jnp.float32)
    for at, part in enumerate(split3(bias_ref[...])):
        part = jnp.broadcast_to(part.astype(jnp.float32), bias_rows.shape)
        bias_rows = jnp.where(row == at, part, bias_rows)
    tail = jnp.concatenate([w_input_ref[...].astype(jnp.float32), bias_rows], axis=0)
    for gate in range(4):
        piece = tail[:, gate * state : (gate + 1) * state] * (1.0 if gate == 2 else 0.5)
        table[gate * state : (gate + 1) * state, state : 2 * state] = piece.T.astype(jnp.bfloat16)
    row = lax.broadcasted_iota(jnp.int32, (PAD, state), 0)
    head_rows = jnp.zeros((PAD, state), jnp.float32)
    for at, part in enumerate(split3(head_ref[...] * 0.5)):
        part = jnp.broadcast_to(part.astype(jnp.float32), head_rows.shape)
        head_rows = jnp.where(row == at, part, head_rows)
    table[gates : gates + PAD, 0:state] = head_rows.astype(jnp.bfloat16)
    copies[6].wait()
    square[0:steps, 0 : release_ref.shape[1]] = release_ref[...]
    given_ref[...] = square[...].T[0 : given_ref.shape[0]]
    for copy in copies[4:6]:
        copy.wait()
    hidden[...] = hidden[...] + hidden[...]
    ones = jnp.ones((PAD, chunk), jnp.bfloat16)

    def step(now, carry):
        frame(now).wait()
        for first in range(0, units, chunk):
            cols = pl.ds(first, chunk)
            operand = jnp.concatenate([hidden[:, cols], forcing_ref[now, :, cols], ones], axis=0)
            total = jnp.dot(table[:, 0:depth], operand, preferred_element_type=jnp.float32)
            head_sum[pl.ds((now + PAD - 1) % PAD, 1), cols] = (
                total[gates : gates + 1] + total[gates + 1 : gates + 2] + total[gates + 2 : gates + 3]
            )
            in_gate = jnp.tanh(total[0:state]) + 1.0
            forget = jnp.tanh(total[state : 2 * state]) + 1.0
            candidate = jnp.tanh(total[2 * state : 3 * state])
            out_gate = jnp.tanh(total[3 * state : 4 * state]) + 1.0
            after = (forget * cell[:, cols] + in_gate * candidate) * 0.5
            cell[:, cols] = after
            hidden[:, cols] = (out_gate * jnp.tanh(after)).astype(jnp.bfloat16)
        return carry

    lax.fori_loop(0, steps, step, 0)
    last = jnp.dot(table[gates : gates + PAD, 0:state], hidden[...], preferred_element_type=jnp.float32)
    head_sum[steps - 1 : steps, :] = last[0:1] + last[1:2] + last[2:3]
    runoff_ref[...] = jax.nn.softplus(head_sum[...]).astype(jnp.bfloat16)
    for copy in copies[7:]:
        copy.wait()


def remap_kernel(
    dest_ref,
    block_ref,
    runoff_ref,
    weight_ref,
    share_ref,
    keep_ref,
    send_ref,
    shift_ref,
    slots,
    square,
    *,
    size,
    reach_blocks,
    steps,
):
    unit_blocks, fan_out, block, _ = weight_ref.shape
    me = lax.axis_index("basin")
    slots[...] = jnp.zeros_like(slots)
    square[...] = jnp.zeros_like(square)
    for group in range(unit_blocks):
        left = runoff_ref[:, group * block : (group + 1) * block]
        for k in range(fan_out):
            contrib = jnp.dot(left, weight_ref[group, k], preferred_element_type=jnp.float32)
            slot = slot_of(dest_ref[group, k] ^ me, size) * reach_blocks + block_ref[group, k]
            slots[slot] = slots[slot] + contrib
    half = size // 2
    rows = reach_blocks * steps
    lane = lax.broadcasted_iota(jnp.int32, (PAD, block), 1)
    row = lax.broadcasted_iota(jnp.int32, (PAD, 1), 0)
    origin = lax.axis_index("unit") * PAD

    def gather(at, out_ref, base, columns):
        pieces = [slots[at * reach_blocks + blk] for blk in range(reach_blocks)]
        tile = jnp.concatenate([piece[0:steps] for piece in pieces], axis=0)
        out_ref[pl.ds((at - base) * rows, rows), :] = tile.astype(jnp.bfloat16)
        section = slot_of(at, size) ^ me
        share = share_ref[section]
        total = pieces[0] * share[0:1]
        for blk in range(1, reach_blocks):
            total = total + pieces[blk] * share[blk : blk + 1]
        column = jnp.sum(total, axis=1, keepdims=True)
        column = jnp.where(row == steps, share[reach_blocks : reach_blocks + 1, 0:1], column)
        column = jnp.where(row > steps, 0.0, column)
        return jnp.where(lane == section, column, columns)

    columns = jnp.zeros((PAD, block), jnp.float32)
    if size <= 16:
        for at in range(size):
            columns = gather(at, keep_ref if at < half else send_ref, 0 if at < half else half, columns)
    else:
        columns = lax.fori_loop(0, half, lambda at, c: gather(at, keep_ref, 0, c), columns)
        columns = lax.fori_loop(half, size, lambda at, c: gather(at, send_ref, half, c), columns)
    square[pl.ds(pl.multiple_of(origin, PAD), PAD), :] = columns
    shift = square[...].T[0:size]
    shift_ref[...] = shift
    high = shift.astype(jnp.bfloat16)
    send_ref[half * rows : half * rows + size, :] = high
    send_ref[half * rows + size : half * rows + 2 * size, :] = (shift - high.astype(jnp.float32)).astype(jnp.bfloat16)


def finish_kernel(
    count_ref,
    parent_ref,
    reservoir_ref,
    given_ref,
    shift_ref,
    mine_ref,
    got_ref,
    route_ref,
    gain_ref,
    out_ref,
    inflow,
    joined,
    *,
    steps,
    unit_size,
):
    reach_blocks, block = gain_ref.shape
    size = shift_ref.shape[0]
    basin, unit = lax.axis_index("basin"), lax.axis_index("unit")
    rows = reach_blocks * steps
    high = got_ref[rows : rows + size, :].astype(jnp.float32)
    total = shift_ref[...] + (high + got_ref[rows + size : rows + 2 * size, :].astype(jnp.float32))
    lateral = mine_ref[...].astype(jnp.float32) + got_ref[0:rows, :].astype(jnp.float32)
    flows = []
    for blk in range(reach_blocks):
        flows.append(
            lax.dot_general(
                lateral[blk * steps : (blk + 1) * steps], route_ref[blk], (((1,), (1,)), ((), ())),
                precision=PRECISE, preferred_element_type=jnp.float32,
            )
        )
    shift = jnp.zeros_like(total)
    factor = jnp.ones_like(total)
    for at in range(unit_size):
        own = jnp.broadcast_to(total[:, at * PAD + steps : at * PAD + steps + 1], total.shape)
        moved = total if at == 0 else pltpu.roll(total, block - at * PAD, 1)
        shift = moved + own * shift
        factor = factor * own
        joined[at, 0] = moved
        joined[at, 1] = own
    joined[unit_size, 0] = shift
    joined[unit_size, 1] = factor
    inflow[...] = jnp.zeros_like(inflow)

    def tree(section):
        at = pl.ds(section, 1)
        outflow = joined[unit_size, 0, at, :] + joined[unit_size, 1, at, :] * inflow[at, :]
        passed = jnp.where(reservoir_ref[section] == 1, given_ref[at, :], outflow)
        parent = pl.ds(parent_ref[section], 1)
        inflow[parent, :] = inflow[parent, :] + passed

    repeat(size, tree)
    here = pl.ds(basin, 1)
    head = inflow[here, :]
    for at in range(unit_size - 1):
        head = jnp.where(at < unit, joined[at, 0, here, :] + joined[at, 1, here, :] * head, head)
    lane = lax.broadcasted_iota(jnp.int32, (PAD, block), 1)
    row = lax.broadcasted_iota(jnp.int32, (PAD, block), 0)
    column = jnp.sum(jnp.where(lane == row, jnp.broadcast_to(head, lane.shape), 0.0), axis=1, keepdims=True)
    carry = jnp.broadcast_to(column[0:steps], (steps, block))
    count = count_ref[basin]
    for blk in range(reach_blocks):
        live = unit * reach_blocks + blk < count
        flow = flows[blk] + carry * gain_ref[blk : blk + 1, :]
        out_ref[:, blk * block : (blk + 1) * block] = jnp.where(live, flow, 0.0)
        carry = jnp.where(live, jnp.broadcast_to(flow[:, block - 1 : block], carry.shape), carry)


def halves(shift):
    high = lax.reduce_precision(shift, 8, 7)
    return [high.astype(jnp.bfloat16), lax.reduce_precision(shift - high, 8, 7).astype(jnp.bfloat16)]


def shards(
    forcing,
    hidden_init,
    cell_init,
    w_input,
    w_recur,
    gate_bias,
    w_head,
    remap_dest,
    remap_block,
    remap_weight,
    route_kernel,
    carry_gain,
    block_count,
    parent_section,
    reservoir,
    release,
):
    steps, features, units = forcing.shape
    state = hidden_init.shape[0]
    gates = 4 * state
    reach_blocks, block, _ = route_kernel.shape
    size, unit_size = lax.axis_size("basin"), lax.axis_size("unit")
    rows = reach_blocks * steps
    like = lambda x: pltpu.VMEM(x.shape, x.dtype)
    params = pltpu.CompilerParams(vmem_limit_bytes=(8 << 20) + (size << 18))

    share = pl.pallas_call(
        functools.partial(prep_kernel, size=size),
        out_shape=jax.ShapeDtypeStruct((size, PAD, block), jnp.float32),
        in_specs=[HBM] * 3,
        out_specs=VMEM,
        scratch_shapes=[
            pltpu.VMEM((reach_blocks, block), jnp.float32),
            pltpu.VMEM((reach_blocks, block), jnp.float32),
            pltpu.SMEM(block_count.shape, jnp.int32),
            pltpu.SemaphoreType.DMA((3,)),
        ],
        compiler_params=params,
        name="prep",
    )(*in_hbm(block_count, route_kernel, carry_gain))
    shares = lax.all_to_all(share, "basin", split_axis=0, concat_axis=0, tiled=True)
    runoff, weight_v, route_v, gain_v, given = pl.pallas_call(
        functools.partial(lstm_kernel, chunk=256),
        out_shape=(
            pltpu.VMEM((PAD, units), jnp.bfloat16),
            like(remap_weight),
            like(route_kernel),
            like(carry_gain),
            pltpu.VMEM((size, block), jnp.float32),
        ),
        in_specs=[HBM] * 11,
        out_specs=(VMEM,) * 5,
        scratch_shapes=[
            pltpu.VMEM((gates, state), jnp.bfloat16),
            pltpu.VMEM((features, gates), jnp.bfloat16),
            pltpu.VMEM((1, gates), jnp.float32),
            pltpu.VMEM((1, state), jnp.float32),
            pltpu.VMEM((state, units), jnp.bfloat16),
            pltpu.VMEM((state, units), jnp.float32),
            pltpu.VMEM(release.shape, jnp.float32),
            pltpu.VMEM((steps, features, units), jnp.bfloat16),
            pltpu.VMEM((gates + PAD, 2 * state), jnp.bfloat16),
            pltpu.VMEM((PAD, units), jnp.float32),
            pltpu.VMEM((block, block), jnp.float32),
            pltpu.SemaphoreType.DMA((steps,)),
            pltpu.SemaphoreType.DMA((10,)),
        ],
        compiler_params=params,
        cost_estimate=pl.CostEstimate(
            flops=2 * steps * gates * (state + features) * units,
            bytes_accessed=4 << 20,
            transcendentals=5 * steps * state * units,
        ),
        name="lstm",
    )(
        *in_hbm(
            w_recur,
            w_input.T,
            gate_bias.reshape(1, gates),
            w_head.reshape(1, state),
            hidden_init,
            cell_init,
            release,
            forcing,
            remap_weight,
            route_kernel,
            carry_gain,
        )
    )
    keep, send, shift = pl.pallas_call(
        functools.partial(remap_kernel, size=size, reach_blocks=reach_blocks, steps=steps),
        out_shape=(
            pltpu.VMEM((size // 2 * rows, block), jnp.bfloat16),
            pltpu.VMEM((size // 2 * rows + 2 * size, block), jnp.bfloat16),
            pltpu.VMEM((size, block), jnp.float32),
        ),
        in_specs=[SMEM, SMEM] + [VMEM] * 3,
        out_specs=(VMEM,) * 3,
        scratch_shapes=[
            pltpu.VMEM((size * reach_blocks, PAD, block), jnp.float32),
            pltpu.VMEM((block, block), jnp.float32),
        ],
        compiler_params=params,
        name="remap",
    )(remap_dest, remap_block, *in_vmem(runoff, weight_v), shares)

    wide = jnp.float32
    exchange = [(at, bit) for at, bit in enumerate(stage_bits(size))]
    across_at = min(1, len(exchange) - 1)
    for at, bit in exchange:
        if at > 0:
            kept = keep.shape[0]
            total = (keep.astype(wide) + got[:kept].astype(wide)).astype(jnp.bfloat16)
            shift = shift + (got[kept : kept + size].astype(wide) + got[kept + size :].astype(wide))
            for part in others:
                shift = shift + part
            keep, send = total[: kept // 2], jnp.concatenate([total[kept // 2 :]] + halves(shift), axis=0)
        swap = 1 << bit
        got = lax.ppermute(send, "basin", [(i, i ^ swap) for i in range(size)])
        others = []
        if at == across_at:
            for turn in range(1, unit_size):
                for hop in (0, swap):
                    route = [
                        (b * unit_size + u, (b ^ hop) * unit_size + (u ^ turn))
                        for b in range(size)
                        for u in range(unit_size)
                    ]
                    others.append(lax.ppermute(shift, AXES, route))
    for part in others:
        shift = shift + part
    return pl.pallas_call(
        functools.partial(finish_kernel, steps=steps, unit_size=unit_size),
        out_shape=jax.ShapeDtypeStruct((steps, reach_blocks * block), jnp.float32),
        in_specs=[SMEM, SMEM, SMEM] + [VMEM] * 6,
        out_specs=VMEM,
        scratch_shapes=[
            pltpu.VMEM((size + 8, block), jnp.float32),
            pltpu.VMEM((unit_size + 1, 2, size, block), jnp.float32),
        ],
        compiler_params=params,
        name="finish",
    )(block_count, parent_section, reservoir, *in_vmem(given), shift, keep, got, *in_vmem(route_v, gain_v))


def solution(mesh):
    placed = (
        P(None, None, AXES),
        P(None, AXES),
        P(None, AXES),
        P(),
        P(),
        P(),
        P(),
        P(AXES, None),
        P(AXES, None),
        P(AXES, None, None, None),
        P(AXES, None, None),
        P(AXES, None),
        P(),
        P(),
        P(),
        P(),
    )
    return jax.shard_map(
        shards, mesh=mesh, in_specs=placed, out_specs=P(None, AXES), check_vma=False
    )
```

```python
import functools

import jax
import jax.numpy as jnp
from jax import lax
from jax.experimental import pallas as pl
from jax.experimental.pallas import tpu as pltpu
from jax.sharding import PartitionSpec as P

PRECISE = lax.Precision.HIGHEST
AXES = ("basin", "unit")
PAD = 16
VMEM = pl.BlockSpec(memory_space=pltpu.VMEM)
SMEM = pl.BlockSpec(memory_space=pltpu.SMEM)
HBM = pl.BlockSpec(memory_space=pltpu.HBM)


def in_hbm(*arrays):
    return [pltpu.with_memory_space_constraint(x, pltpu.HBM) for x in arrays]


def in_vmem(*arrays):
    return [pltpu.with_memory_space_constraint(x, pltpu.VMEM) for x in arrays]


def stage_bits(size):
    return range(size.bit_length() - 1)


def slot_of(relative, size):
    slot = relative * 0
    for bit in stage_bits(size):
        slot = slot * 2 + ((relative >> bit) & 1)
    return slot


def split3(x):
    high = x.astype(jnp.bfloat16)
    rest = x - high.astype(jnp.float32)
    middle = rest.astype(jnp.bfloat16)
    low = (rest - middle.astype(jnp.float32)).astype(jnp.bfloat16)
    return high, middle, low


def repeat(count, body):
    if count <= 16:
        for at in range(count):
            body(at)
    else:
        lax.fori_loop(0, count, lambda at, carry: (body(at), carry)[1], 0)


def prep_kernel(count_hbm, route_hbm, gain_hbm, share_ref, last_ref, gain_ref, count_ref, sems, *, size):
    reach_blocks, block = gain_hbm.shape
    copies = [
        pltpu.make_async_copy(route_hbm.at[:, block - 1, :], last_ref, sems.at[0]),
        pltpu.make_async_copy(gain_hbm, gain_ref, sems.at[1]),
        pltpu.make_async_copy(count_hbm, count_ref, sems.at[2]),
    ]
    for copy in copies:
        copy.start()
    for copy in copies:
        copy.wait()
    first = lax.axis_index("unit") * reach_blocks
    count = count_ref[lax.axis_index("basin")]
    factor = jnp.ones((1, block), jnp.float32)
    rows = [None] * reach_blocks
    for blk in reversed(range(reach_blocks)):
        live = first + blk < count
        rows[blk] = jnp.where(live, factor * last_ref[blk : blk + 1, :], 0.0)
        ratio = jnp.broadcast_to(gain_ref[blk : blk + 1, block - 1 : block], (1, block))
        factor = jnp.where(live, factor * ratio, factor)
    rows.append(factor * (1.0 / size))
    rows.append(jnp.zeros((PAD - len(rows), block), jnp.float32))
    share_ref[...] = jnp.concatenate(rows, axis=0)


def advance(table, frame, hidden, cell, hidden_out, cell_out, head_row, *, chunk):
    state, units = hidden.shape
    depth = state + frame.shape[0] + PAD
    ones = jnp.ones((PAD, chunk), jnp.bfloat16)
    for first in range(0, units, chunk):
        cols = pl.ds(first, chunk)
        operand = jnp.concatenate([hidden[:, cols], frame[:, cols], ones], axis=0)

        def gate(at, rows=state):
            piece = table[at * state : at * state + rows, 0:depth]
            return jnp.dot(piece, operand, preferred_element_type=jnp.float32)

        if head_row is not None:
            head = gate(4, PAD)
            head_row[:, cols] = head[0:1] + head[1:2] + head[2:3]
        kept = (jnp.tanh(gate(1)) + 1.0) * cell[:, cols]
        taken = (jnp.tanh(gate(0)) + 1.0) * jnp.tanh(gate(2))
        after = (kept + taken) * 0.5
        cell_out[:, cols] = after
        hidden_out[:, cols] = ((jnp.tanh(gate(3)) + 1.0) * jnp.tanh(after)).astype(jnp.bfloat16)


def build_table(table, w_recur_ref, w_input_ref, bias_ref, head_ref):
    gates, state = w_recur_ref.shape
    features = w_input_ref.shape[0]
    table[gates : gates + PAD, state : 2 * state] = jnp.zeros((PAD, state), jnp.bfloat16)
    for gate in range(4):
        at = pl.ds(gate * state, state)
        scale = 0.5 if gate == 2 else 0.25
        table[at, 0:state] = (w_recur_ref[at, :].astype(jnp.float32) * scale).astype(jnp.bfloat16)
    row = lax.broadcasted_iota(jnp.int32, (state - features, gates), 0)
    bias_rows = jnp.zeros((state - features, gates), jnp.float32)
    for at, part in enumerate(split3(bias_ref[...])):
        part = jnp.broadcast_to(part.astype(jnp.float32), bias_rows.shape)
        bias_rows = jnp.where(row == at, part, bias_rows)
    tail = jnp.concatenate([w_input_ref[...].astype(jnp.float32), bias_rows], axis=0)
    for gate in range(4):
        piece = tail[:, gate * state : (gate + 1) * state] * (1.0 if gate == 2 else 0.5)
        table[gate * state : (gate + 1) * state, state : 2 * state] = piece.T.astype(jnp.bfloat16)
    row = lax.broadcasted_iota(jnp.int32, (PAD, state), 0)
    head_rows = jnp.zeros((PAD, state), jnp.float32)
    for at, part in enumerate(split3(head_ref[...] * 0.5)):
        part = jnp.broadcast_to(part.astype(jnp.float32), head_rows.shape)
        head_rows = jnp.where(row == at, part, head_rows)
    table[gates : gates + PAD, 0:state] = head_rows.astype(jnp.bfloat16)


def first_kernel(
    w_recur_hbm,
    w_input_hbm,
    bias_hbm,
    head_hbm,
    hidden_hbm,
    cell_hbm,
    release_hbm,
    forcing_hbm,
    forcing_ref,
    table,
    hidden,
    cell,
    head_sum,
    given_ref,
    w_recur_ref,
    w_input_ref,
    bias_ref,
    head_ref,
    release_ref,
    square,
    frame_sems,
    sems,
    *,
    count,
    chunk,
):
    steps = forcing_hbm.shape[0]
    pairs = [
        (w_recur_hbm, w_recur_ref),
        (w_input_hbm, w_input_ref),
        (bias_hbm, bias_ref),
        (head_hbm, head_ref),
        (release_hbm, release_ref),
        (hidden_hbm, hidden),
        (cell_hbm, cell),
    ]
    copies = [pltpu.make_async_copy(a, b, sems.at[at]) for at, (a, b) in enumerate(pairs)]
    frames = [
        pltpu.make_async_copy(forcing_hbm.at[now], forcing_ref.at[now], frame_sems.at[now])
        for now in range(steps)
    ]
    for copy in copies + frames:
        copy.start()
    square[...] = jnp.zeros_like(square)
    head_sum[...] = jnp.zeros_like(head_sum)
    for copy in copies[:5]:
        copy.wait()
    build_table(table, w_recur_ref, w_input_ref, bias_ref, head_ref)
    square[0:steps, 0 : release_ref.shape[1]] = release_ref[...]
    given_ref[...] = square[...].T[0 : given_ref.shape[0]]
    for copy in copies[5:]:
        copy.wait()
    hidden[...] = hidden[...] + hidden[...]
    for now in range(count):
        frames[now].wait()
        row = head_sum.at[now - 1 : now] if now > 0 else None
        advance(table, forcing_ref.at[now], hidden, cell, hidden, cell, row, chunk=chunk)
    for now in range(count, steps):
        frames[now].wait()


def later_kernel(*refs, first, count, last, fetched, chunk):
    forcing_ref, table, hidden_in, cell_in, head_in = refs[:5]
    sources, refs = refs[6 : 6 + fetched], refs[6 + fetched :]
    if last:
        runoff_ref, refs = refs[0], refs[1:]
    else:
        (hidden, cell, head_sum), refs = refs[:3], refs[3:]
    targets, refs = refs[:fetched], refs[fetched:]
    if last:
        hidden, cell, head_sum, sems = refs
    else:
        (sems,) = refs
    copies = [pltpu.make_async_copy(a, b, sems.at[at]) for at, (a, b) in enumerate(zip(sources, targets))]
    for copy in copies:
        copy.start()
    state = hidden_in.shape[0]
    gates = 4 * state
    head_sum[...] = head_in[...]
    for now in range(first, first + count):
        begin = now == first
        row = head_sum.at[now - 1 : now]
        old = (hidden_in, cell_in) if begin else (hidden, cell)
        advance(table, forcing_ref.at[now], *old, hidden, cell, row, chunk=chunk)
    if last:
        end = jnp.dot(table[gates : gates + PAD, 0:state], hidden[...], preferred_element_type=jnp.float32)
        now = first + count
        head_sum[now - 1 : now, :] = end[0:1] + end[1:2] + end[2:3]
        runoff_ref[...] = jax.nn.softplus(head_sum[...]).astype(jnp.bfloat16)
    for copy in copies:
        copy.wait()


def remap_kernel(
    dest_ref,
    block_ref,
    runoff_ref,
    weight_ref,
    share_ref,
    keep_ref,
    send_ref,
    shift_ref,
    slots,
    square,
    *,
    size,
    reach_blocks,
    steps,
):
    unit_blocks, fan_out, block, _ = weight_ref.shape
    me = lax.axis_index("basin")
    slots[...] = jnp.zeros_like(slots)
    square[...] = jnp.zeros_like(square)
    for group in range(unit_blocks):
        left = runoff_ref[:, group * block : (group + 1) * block]
        for k in range(fan_out):
            contrib = jnp.dot(left, weight_ref[group, k], preferred_element_type=jnp.float32)
            slot = slot_of(dest_ref[group, k] ^ me, size) * reach_blocks + block_ref[group, k]
            slots[slot] = slots[slot] + contrib
    half = size // 2
    rows = reach_blocks * steps
    lane = lax.broadcasted_iota(jnp.int32, (PAD, block), 1)
    row = lax.broadcasted_iota(jnp.int32, (PAD, 1), 0)
    origin = lax.axis_index("unit") * PAD

    def gather(at, out_ref, base, columns):
        pieces = [slots[at * reach_blocks + blk] for blk in range(reach_blocks)]
        tile = jnp.concatenate([piece[0:steps] for piece in pieces], axis=0)
        out_ref[pl.ds((at - base) * rows, rows), :] = tile.astype(jnp.bfloat16)
        relative = slot_of(at, size)
        section = relative ^ me
        share = share_ref[relative]
        total = pieces[0] * share[0:1]
        for blk in range(1, reach_blocks):
            total = total + pieces[blk] * share[blk : blk + 1]
        column = jnp.sum(total, axis=1, keepdims=True)
        column = jnp.where(row == steps, share[reach_blocks : reach_blocks + 1, 0:1], column)
        column = jnp.where(row > steps, 0.0, column)
        return jnp.where(lane == section, column, columns)

    columns = jnp.zeros((PAD, block), jnp.float32)
    if size <= 16:
        for at in range(size):
            columns = gather(at, keep_ref if at < half else send_ref, 0 if at < half else half, columns)
    else:
        columns = lax.fori_loop(0, half, lambda at, c: gather(at, keep_ref, 0, c), columns)
        columns = lax.fori_loop(half, size, lambda at, c: gather(at, send_ref, half, c), columns)
    square[pl.ds(pl.multiple_of(origin, PAD), PAD), :] = columns
    shift = square[...].T[0:size]
    shift_ref[...] = shift
    high = shift.astype(jnp.bfloat16)
    send_ref[half * rows : half * rows + size, :] = high
    send_ref[half * rows + size : half * rows + 2 * size, :] = (shift - high.astype(jnp.float32)).astype(jnp.bfloat16)


def finish_kernel(
    count_ref,
    parent_ref,
    reservoir_ref,
    given_ref,
    shift_ref,
    mine_ref,
    got_ref,
    route_ref,
    gain_ref,
    out_ref,
    inflow,
    joined,
    *,
    steps,
    unit_size,
):
    reach_blocks, block = gain_ref.shape
    size = shift_ref.shape[0]
    basin, unit = lax.axis_index("basin"), lax.axis_index("unit")
    rows = reach_blocks * steps
    high = got_ref[rows : rows + size, :].astype(jnp.float32)
    total = shift_ref[...] + (high + got_ref[rows + size : rows + 2 * size, :].astype(jnp.float32))
    lateral = mine_ref[...].astype(jnp.float32) + got_ref[0:rows, :].astype(jnp.float32)
    flows = []
    for blk in range(reach_blocks):
        flows.append(
            lax.dot_general(
                lateral[blk * steps : (blk + 1) * steps], route_ref[blk], (((1,), (1,)), ((), ())),
                precision=PRECISE, preferred_element_type=jnp.float32,
            )
        )
    shift = jnp.zeros_like(total)
    factor = jnp.ones_like(total)
    for at in range(unit_size):
        own = jnp.broadcast_to(total[:, at * PAD + steps : at * PAD + steps + 1], total.shape)
        moved = total if at == 0 else pltpu.roll(total, block - at * PAD, 1)
        shift = moved + own * shift
        factor = factor * own
        joined[at, 0] = moved
        joined[at, 1] = own
    joined[unit_size, 0] = shift
    joined[unit_size, 1] = factor
    inflow[...] = jnp.zeros_like(inflow)

    def tree(section):
        at = pl.ds(section, 1)
        outflow = joined[unit_size, 0, at, :] + joined[unit_size, 1, at, :] * inflow[at, :]
        passed = jnp.where(reservoir_ref[section] == 1, given_ref[at, :], outflow)
        parent = pl.ds(parent_ref[section], 1)
        inflow[parent, :] = inflow[parent, :] + passed

    repeat(size, tree)
    here = pl.ds(basin, 1)
    head = inflow[here, :]
    for at in range(unit_size - 1):
        head = jnp.where(at < unit, joined[at, 0, here, :] + joined[at, 1, here, :] * head, head)
    lane = lax.broadcasted_iota(jnp.int32, (PAD, block), 1)
    row = lax.broadcasted_iota(jnp.int32, (PAD, block), 0)
    column = jnp.sum(jnp.where(lane == row, jnp.broadcast_to(head, lane.shape), 0.0), axis=1, keepdims=True)
    carry = jnp.broadcast_to(column[0:steps], (steps, block))
    count = count_ref[basin]
    for blk in range(reach_blocks):
        live = unit * reach_blocks + blk < count
        flow = flows[blk] + carry * gain_ref[blk : blk + 1, :]
        out_ref[:, blk * block : (blk + 1) * block] = jnp.where(live, flow, 0.0)
        carry = jnp.where(live, jnp.broadcast_to(flow[:, block - 1 : block], carry.shape), carry)


def halves(shift):
    high = lax.reduce_precision(shift, 8, 7)
    return [high.astype(jnp.bfloat16), lax.reduce_precision(shift - high, 8, 7).astype(jnp.bfloat16)]


def shards(
    forcing,
    hidden_init,
    cell_init,
    w_input,
    w_recur,
    gate_bias,
    w_head,
    remap_dest,
    remap_block,
    remap_weight,
    route_kernel,
    carry_gain,
    block_count,
    parent_section,
    reservoir,
    release,
):
    steps, features, units = forcing.shape
    state = hidden_init.shape[0]
    gates = 4 * state
    reach_blocks, block, _ = route_kernel.shape
    size, unit_size = lax.axis_size("basin"), lax.axis_size("unit")
    rows = reach_blocks * steps
    like = lambda x: pltpu.VMEM(x.shape, x.dtype)
    params = pltpu.CompilerParams(vmem_limit_bytes=(8 << 20) + (size << 18))

    share = pl.pallas_call(
        functools.partial(prep_kernel, size=size),
        out_shape=pltpu.VMEM((PAD, block), jnp.float32),
        in_specs=[HBM] * 3,
        out_specs=VMEM,
        scratch_shapes=[
            pltpu.VMEM((reach_blocks, block), jnp.float32),
            pltpu.VMEM((reach_blocks, block), jnp.float32),
            pltpu.SMEM(block_count.shape, jnp.int32),
            pltpu.SemaphoreType.DMA((3,)),
        ],
        compiler_params=params,
        name="prep",
    )(*in_hbm(block_count, route_kernel, carry_gain))
    shares = share[None]
    order = []
    for bit in stage_bits(size):
        other = lax.ppermute(shares, "basin", [(i, i ^ (1 << bit)) for i in range(size)])
        order.append(other)
        shares = jnp.concatenate([shares, other], axis=0)

    chunk = 256
    parts = 4
    bounds = [0] + [1 + (steps - 1) * part // (parts - 1) for part in range(parts)]
    carried = (
        pltpu.VMEM((state, units), jnp.bfloat16),
        pltpu.VMEM((state, units), jnp.float32),
        pltpu.VMEM((PAD, units), jnp.float32),
    )

    def cost(count):
        return pl.CostEstimate(
            flops=2 * count * gates * (state + features) * units,
            bytes_accessed=4 << 20,
            transcendentals=5 * count * state * units,
        )

    forcing_v, table, hidden, cell, head_sum, given = pl.pallas_call(
        functools.partial(first_kernel, count=bounds[1], chunk=chunk),
        out_shape=(
            like(forcing),
            pltpu.VMEM((gates + PAD, 2 * state), jnp.bfloat16),
            *carried,
            pltpu.VMEM((size, block), jnp.float32),
        ),
        in_specs=[HBM] * 8,
        out_specs=(VMEM,) * 6,
        scratch_shapes=[
            pltpu.VMEM((gates, state), jnp.bfloat16),
            pltpu.VMEM((features, gates), jnp.bfloat16),
            pltpu.VMEM((1, gates), jnp.float32),
            pltpu.VMEM((1, state), jnp.float32),
            pltpu.VMEM(release.shape, jnp.float32),
            pltpu.VMEM((block, block), jnp.float32),
            pltpu.SemaphoreType.DMA((steps,)),
            pltpu.SemaphoreType.DMA((7,)),
        ],
        compiler_params=params,
        cost_estimate=cost(bounds[1]),
        name="lstm0",
    )(
        *in_hbm(
            w_recur,
            w_input.T,
            gate_bias.reshape(1, gates),
            w_head.reshape(1, state),
            hidden_init,
            cell_init,
            release,
            forcing,
        )
    )
    for part in range(1, parts):
        last = part == parts - 1
        fetch = {1: (route_kernel, carry_gain), parts - 1: (remap_weight,)}.get(part, ())
        results = (pltpu.VMEM((PAD, units), jnp.bfloat16),) if last else carried
        outs = pl.pallas_call(
            functools.partial(
                later_kernel,
                first=bounds[part],
                count=bounds[part + 1] - bounds[part],
                last=last,
                fetched=len(fetch),
                chunk=chunk,
            ),
            out_shape=results + tuple(like(x) for x in fetch),
            in_specs=[VMEM] * 5 + [pl.BlockSpec(memory_space=pl.ANY)] + [HBM] * len(fetch),
            out_specs=(VMEM,) * (len(results) + len(fetch)),
            scratch_shapes=(list(carried) if last else []) + [pltpu.SemaphoreType.DMA((max(1, len(fetch)),))],
            compiler_params=params,
            cost_estimate=cost(bounds[part + 1] - bounds[part]),
            name=f"lstm{part}",
        )(
            *in_vmem(forcing_v, table, hidden, cell, head_sum),
            order[min(part, len(order)) - 1],
            *in_hbm(*fetch),
        )
        if part == 1:
            route_v, gain_v = outs[len(results) :]
        if last:
            runoff, weight_v = outs
        else:
            hidden, cell, head_sum = outs[:3]
    keep, send, shift = pl.pallas_call(
        functools.partial(remap_kernel, size=size, reach_blocks=reach_blocks, steps=steps),
        out_shape=(
            pltpu.VMEM((size // 2 * rows, block), jnp.bfloat16),
            pltpu.VMEM((size // 2 * rows + 2 * size, block), jnp.bfloat16),
            pltpu.VMEM((size, block), jnp.float32),
        ),
        in_specs=[SMEM, SMEM] + [VMEM] * 3,
        out_specs=(VMEM,) * 3,
        scratch_shapes=[
            pltpu.VMEM((size * reach_blocks, PAD, block), jnp.float32),
            pltpu.VMEM((block, block), jnp.float32),
        ],
        compiler_params=params,
        name="remap",
    )(remap_dest, remap_block, *in_vmem(runoff, weight_v), shares)

    wide = jnp.float32
    exchange = [(at, bit) for at, bit in enumerate(stage_bits(size))]
    across_at = min(1, len(exchange) - 1)
    for at, bit in exchange:
        if at > 0:
            kept = keep.shape[0]
            total = (keep.astype(wide) + got[:kept].astype(wide)).astype(jnp.bfloat16)
            shift = shift + (got[kept : kept + size].astype(wide) + got[kept + size :].astype(wide))
            for part in others:
                shift = shift + part
            keep, send = total[: kept // 2], jnp.concatenate([total[kept // 2 :]] + halves(shift), axis=0)
        swap = 1 << bit
        got = lax.ppermute(send, "basin", [(i, i ^ swap) for i in range(size)])
        others = []
        if at == across_at:
            for turn in range(1, unit_size):
                for hop in (0, swap):
                    route = [
                        (b * unit_size + u, (b ^ hop) * unit_size + (u ^ turn))
                        for b in range(size)
                        for u in range(unit_size)
                    ]
                    others.append(lax.ppermute(shift, AXES, route))
    for part in others:
        shift = shift + part
    return pl.pallas_call(
        functools.partial(finish_kernel, steps=steps, unit_size=unit_size),
        out_shape=jax.ShapeDtypeStruct((steps, reach_blocks * block), jnp.float32),
        in_specs=[SMEM, SMEM, SMEM] + [VMEM] * 6,
        out_specs=VMEM,
        scratch_shapes=[
            pltpu.VMEM((size + 8, block), jnp.float32),
            pltpu.VMEM((unit_size + 1, 2, size, block), jnp.float32),
        ],
        compiler_params=params,
        name="finish",
    )(block_count, parent_section, reservoir, *in_vmem(given), shift, keep, got, *in_vmem(route_v, gain_v))


def solution(mesh):
    placed = (
        P(None, None, AXES),
        P(None, AXES),
        P(None, AXES),
        P(),
        P(),
        P(),
        P(),
        P(AXES, None),
        P(AXES, None),
        P(AXES, None, None, None),
        P(AXES, None, None),
        P(AXES, None),
        P(),
        P(),
        P(),
        P(),
    )
    return jax.shard_map(
        shards, mesh=mesh, in_specs=placed, out_specs=P(None, AXES), check_vma=False
    )
```

```python
import functools

import jax
import jax.numpy as jnp
from jax import lax
from jax.experimental import pallas as pl
from jax.experimental.pallas import tpu as pltpu
from jax.sharding import PartitionSpec as P

PRECISE = lax.Precision.HIGHEST
AXES = ("basin", "unit")
PAD = 16
VMEM = pl.BlockSpec(memory_space=pltpu.VMEM)
SMEM = pl.BlockSpec(memory_space=pltpu.SMEM)
HBM = pl.BlockSpec(memory_space=pltpu.HBM)


def in_hbm(*arrays):
    return [pltpu.with_memory_space_constraint(x, pltpu.HBM) for x in arrays]


def in_vmem(*arrays):
    return [pltpu.with_memory_space_constraint(x, pltpu.VMEM) for x in arrays]


def stage_bits(size):
    return range(size.bit_length() - 1)


def gather_bits(size):
    bits = list(range(size.bit_length() - 1))
    return bits[1:] + bits[:1]


def place_of(relative, size):
    return sum(((relative >> bit) & 1) << at for at, bit in enumerate(gather_bits(size)))


def slot_of(relative, size):
    slot = relative * 0
    for bit in stage_bits(size):
        slot = slot * 2 + ((relative >> bit) & 1)
    return slot


def relative_of(slot, size):
    bits = list(stage_bits(size))
    return sum(((slot >> (len(bits) - 1 - at)) & 1) << bit for at, bit in enumerate(bits))


def split3(x):
    high = x.astype(jnp.bfloat16)
    rest = x - high.astype(jnp.float32)
    middle = rest.astype(jnp.bfloat16)
    low = (rest - middle.astype(jnp.float32)).astype(jnp.bfloat16)
    return high, middle, low


def repeat(count, body):
    if count <= 16:
        for at in range(count):
            body(at)
    else:
        lax.fori_loop(0, count, lambda at, carry: (body(at), carry)[1], 0)


def prep_kernel(count_hbm, route_hbm, gain_hbm, share_ref, last_ref, gain_ref, count_ref, sems, *, size):
    reach_blocks, block = gain_hbm.shape
    copies = [
        pltpu.make_async_copy(route_hbm.at[:, block - 1, :], last_ref, sems.at[0]),
        pltpu.make_async_copy(gain_hbm, gain_ref, sems.at[1]),
        pltpu.make_async_copy(count_hbm, count_ref, sems.at[2]),
    ]
    for copy in copies:
        copy.start()
    for copy in copies:
        copy.wait()
    first = lax.axis_index("unit") * reach_blocks
    count = count_ref[lax.axis_index("basin")]
    factor = jnp.ones((1, block), jnp.float32)
    rows = [None] * reach_blocks
    for blk in reversed(range(reach_blocks)):
        live = first + blk < count
        rows[blk] = jnp.where(live, factor * last_ref[blk : blk + 1, :], 0.0)
        ratio = jnp.broadcast_to(gain_ref[blk : blk + 1, block - 1 : block], (1, block))
        factor = jnp.where(live, factor * ratio, factor)
    rows.append(factor * (1.0 / size))
    rows.append(jnp.zeros((PAD - len(rows), block), jnp.float32))
    share_ref[...] = jnp.concatenate(rows, axis=0)


def advance(table, frame, hidden, cell, hidden_out, cell_out, head_row, *, chunk):
    state, units = hidden.shape
    depth = state + frame.shape[0] + PAD
    ones = jnp.ones((PAD, chunk), jnp.bfloat16)
    for first in range(0, units, chunk):
        cols = pl.ds(first, chunk)
        operand = jnp.concatenate([hidden[:, cols], frame[:, cols], ones], axis=0)

        def gate(at, rows=state):
            piece = table[at * state : at * state + rows, 0:depth]
            return jnp.dot(piece, operand, preferred_element_type=jnp.float32)

        if head_row is not None:
            head = gate(4, PAD)
            head_row[:, cols] = head[0:1] + head[1:2] + head[2:3]
        kept = (jnp.tanh(gate(1)) + 1.0) * cell[:, cols]
        taken = (jnp.tanh(gate(0)) + 1.0) * jnp.tanh(gate(2))
        after = (kept + taken) * 0.5
        cell_out[:, cols] = after
        hidden_out[:, cols] = ((jnp.tanh(gate(3)) + 1.0) * jnp.tanh(after)).astype(jnp.bfloat16)


def build_table(table, w_recur_ref, w_input_ref, bias_ref, head_ref):
    gates, state = w_recur_ref.shape
    features = w_input_ref.shape[0]
    table[gates : gates + PAD, state : 2 * state] = jnp.zeros((PAD, state), jnp.bfloat16)
    for gate in range(4):
        at = pl.ds(gate * state, state)
        scale = 0.5 if gate == 2 else 0.25
        table[at, 0:state] = (w_recur_ref[at, :].astype(jnp.float32) * scale).astype(jnp.bfloat16)
    row = lax.broadcasted_iota(jnp.int32, (state - features, gates), 0)
    bias_rows = jnp.zeros((state - features, gates), jnp.float32)
    for at, part in enumerate(split3(bias_ref[...])):
        part = jnp.broadcast_to(part.astype(jnp.float32), bias_rows.shape)
        bias_rows = jnp.where(row == at, part, bias_rows)
    tail = jnp.concatenate([w_input_ref[...].astype(jnp.float32), bias_rows], axis=0)
    for gate in range(4):
        piece = tail[:, gate * state : (gate + 1) * state] * (1.0 if gate == 2 else 0.5)
        table[gate * state : (gate + 1) * state, state : 2 * state] = piece.T.astype(jnp.bfloat16)
    row = lax.broadcasted_iota(jnp.int32, (PAD, state), 0)
    head_rows = jnp.zeros((PAD, state), jnp.float32)
    for at, part in enumerate(split3(head_ref[...] * 0.5)):
        part = jnp.broadcast_to(part.astype(jnp.float32), head_rows.shape)
        head_rows = jnp.where(row == at, part, head_rows)
    table[gates : gates + PAD, 0:state] = head_rows.astype(jnp.bfloat16)


def first_kernel(
    w_recur_hbm,
    w_input_hbm,
    bias_hbm,
    head_hbm,
    hidden_hbm,
    cell_hbm,
    release_hbm,
    forcing_hbm,
    forcing_ref,
    table,
    hidden,
    cell,
    head_sum,
    given_ref,
    w_recur_ref,
    w_input_ref,
    bias_ref,
    head_ref,
    release_ref,
    square,
    frame_sems,
    sems,
    *,
    count,
    chunk,
):
    steps = forcing_hbm.shape[0]
    pairs = [
        (w_recur_hbm, w_recur_ref),
        (w_input_hbm, w_input_ref),
        (bias_hbm, bias_ref),
        (head_hbm, head_ref),
        (release_hbm, release_ref),
        (hidden_hbm, hidden),
        (cell_hbm, cell),
    ]
    copies = [pltpu.make_async_copy(a, b, sems.at[at]) for at, (a, b) in enumerate(pairs)]
    frames = [
        pltpu.make_async_copy(forcing_hbm.at[now], forcing_ref.at[now], frame_sems.at[now])
        for now in range(steps)
    ]
    for copy in copies + frames:
        copy.start()
    square[...] = jnp.zeros_like(square)
    head_sum[...] = jnp.zeros_like(head_sum)
    for copy in copies[:5]:
        copy.wait()
    build_table(table, w_recur_ref, w_input_ref, bias_ref, head_ref)
    square[0:steps, 0 : release_ref.shape[1]] = release_ref[...]
    given_ref[...] = square[...].T[0 : given_ref.shape[0]]
    for copy in copies[5:]:
        copy.wait()
    hidden[...] = hidden[...] + hidden[...]
    for now in range(count):
        frames[now].wait()
        row = head_sum.at[now - 1 : now] if now > 0 else None
        advance(table, forcing_ref.at[now], hidden, cell, hidden, cell, row, chunk=chunk)
    for now in range(count, steps):
        frames[now].wait()


def later_kernel(*refs, first, count, last, fetched, chunk):
    forcing_ref, table, hidden_in, cell_in, head_in = refs[:5]
    sources, refs = refs[6 : 6 + fetched], refs[6 + fetched :]
    if last:
        runoff_ref, refs = refs[0], refs[1:]
    else:
        (hidden, cell, head_sum), refs = refs[:3], refs[3:]
    targets, refs = refs[:fetched], refs[fetched:]
    if last:
        hidden, cell, head_sum, sems = refs
    else:
        (sems,) = refs
    copies = [pltpu.make_async_copy(a, b, sems.at[at]) for at, (a, b) in enumerate(zip(sources, targets))]
    for copy in copies:
        copy.start()
    state = hidden_in.shape[0]
    gates = 4 * state
    head_sum[...] = head_in[...]
    for now in range(first, first + count):
        begin = now == first
        row = head_sum.at[now - 1 : now]
        old = (hidden_in, cell_in) if begin else (hidden, cell)
        advance(table, forcing_ref.at[now], *old, hidden, cell, row, chunk=chunk)
    if last:
        end = jnp.dot(table[gates : gates + PAD, 0:state], hidden[...], preferred_element_type=jnp.float32)
        now = first + count
        head_sum[now - 1 : now, :] = end[0:1] + end[1:2] + end[2:3]
        runoff_ref[...] = jax.nn.softplus(head_sum[...]).astype(jnp.bfloat16)
    for copy in copies:
        copy.wait()


def remap_kernel(
    dest_ref,
    block_ref,
    runoff_ref,
    weight_ref,
    share_ref,
    keep_ref,
    send_ref,
    shift_ref,
    slots,
    square,
    *,
    size,
    reach_blocks,
    steps,
):
    unit_blocks, fan_out, block, _ = weight_ref.shape
    me = lax.axis_index("basin")
    slots[...] = jnp.zeros_like(slots)
    square[...] = jnp.zeros_like(square)
    for group in range(unit_blocks):
        left = runoff_ref[:, group * block : (group + 1) * block]
        for k in range(fan_out):
            contrib = jnp.dot(left, weight_ref[group, k], preferred_element_type=jnp.float32)
            slot = slot_of(dest_ref[group, k] ^ me, size) * reach_blocks + block_ref[group, k]
            slots[slot] = slots[slot] + contrib
    half = size // 2
    rows = reach_blocks * steps
    lane = lax.broadcasted_iota(jnp.int32, (PAD, block), 1)
    row = lax.broadcasted_iota(jnp.int32, (PAD, 1), 0)
    origin = lax.axis_index("unit") * PAD

    def gather(at, out_ref, base, columns):
        pieces = [slots[at * reach_blocks + blk] for blk in range(reach_blocks)]
        tile = jnp.concatenate([piece[0:steps] for piece in pieces], axis=0)
        out_ref[pl.ds((at - base) * rows, rows), :] = tile.astype(jnp.bfloat16)
        relative = relative_of(at, size)
        section = relative ^ me
        share = share_ref[place_of(relative, size)]
        total = pieces[0] * share[0:1]
        for blk in range(1, reach_blocks):
            total = total + pieces[blk] * share[blk : blk + 1]
        column = jnp.sum(total, axis=1, keepdims=True)
        column = jnp.where(row == steps, share[reach_blocks : reach_blocks + 1, 0:1], column)
        column = jnp.where(row > steps, 0.0, column)
        return jnp.where(lane == section, column, columns)

    columns = jnp.zeros((PAD, block), jnp.float32)
    if size <= 16:
        for at in range(size):
            columns = gather(at, keep_ref if at < half else send_ref, 0 if at < half else half, columns)
    else:
        columns = lax.fori_loop(0, half, lambda at, c: gather(at, keep_ref, 0, c), columns)
        columns = lax.fori_loop(half, size, lambda at, c: gather(at, send_ref, half, c), columns)
    square[pl.ds(pl.multiple_of(origin, PAD), PAD), :] = columns
    shift = square[...].T[0:size]
    shift_ref[...] = shift
    high = shift.astype(jnp.bfloat16)
    send_ref[half * rows : half * rows + size, :] = high
    send_ref[half * rows + size : half * rows + 2 * size, :] = (shift - high.astype(jnp.float32)).astype(jnp.bfloat16)


def finish_kernel(
    count_ref,
    parent_ref,
    reservoir_ref,
    given_ref,
    shift_ref,
    mine_ref,
    got_ref,
    route_ref,
    gain_ref,
    out_ref,
    inflow,
    joined,
    *,
    steps,
    unit_size,
):
    reach_blocks, block = gain_ref.shape
    size = shift_ref.shape[0]
    basin, unit = lax.axis_index("basin"), lax.axis_index("unit")
    rows = reach_blocks * steps
    high = got_ref[rows : rows + size, :].astype(jnp.float32)
    total = shift_ref[...] + (high + got_ref[rows + size : rows + 2 * size, :].astype(jnp.float32))
    lateral = mine_ref[...].astype(jnp.float32) + got_ref[0:rows, :].astype(jnp.float32)
    flows = []
    for blk in range(reach_blocks):
        flows.append(
            lax.dot_general(
                lateral[blk * steps : (blk + 1) * steps], route_ref[blk], (((1,), (1,)), ((), ())),
                precision=PRECISE, preferred_element_type=jnp.float32,
            )
        )
    shift = jnp.zeros_like(total)
    factor = jnp.ones_like(total)
    for at in range(unit_size):
        own = jnp.broadcast_to(total[:, at * PAD + steps : at * PAD + steps + 1], total.shape)
        moved = total if at == 0 else pltpu.roll(total, block - at * PAD, 1)
        shift = moved + own * shift
        factor = factor * own
        joined[at, 0] = moved
        joined[at, 1] = own
    joined[unit_size, 0] = shift
    joined[unit_size, 1] = factor
    inflow[...] = jnp.zeros_like(inflow)

    def tree(section):
        at = pl.ds(section, 1)
        outflow = joined[unit_size, 0, at, :] + joined[unit_size, 1, at, :] * inflow[at, :]
        passed = jnp.where(reservoir_ref[section] == 1, given_ref[at, :], outflow)
        parent = pl.ds(parent_ref[section], 1)
        inflow[parent, :] = inflow[parent, :] + passed

    repeat(size, tree)
    here = pl.ds(basin, 1)
    head = inflow[here, :]
    for at in range(unit_size - 1):
        head = jnp.where(at < unit, joined[at, 0, here, :] + joined[at, 1, here, :] * head, head)
    lane = lax.broadcasted_iota(jnp.int32, (PAD, block), 1)
    row = lax.broadcasted_iota(jnp.int32, (PAD, block), 0)
    column = jnp.sum(jnp.where(lane == row, jnp.broadcast_to(head, lane.shape), 0.0), axis=1, keepdims=True)
    carry = jnp.broadcast_to(column[0:steps], (steps, block))
    count = count_ref[basin]
    for blk in range(reach_blocks):
        live = unit * reach_blocks + blk < count
        flow = flows[blk] + carry * gain_ref[blk : blk + 1, :]
        out_ref[:, blk * block : (blk + 1) * block] = jnp.where(live, flow, 0.0)
        carry = jnp.where(live, jnp.broadcast_to(flow[:, block - 1 : block], carry.shape), carry)


def halves(shift):
    high = lax.reduce_precision(shift, 8, 7)
    return [high.astype(jnp.bfloat16), lax.reduce_precision(shift - high, 8, 7).astype(jnp.bfloat16)]


def shards(
    forcing,
    hidden_init,
    cell_init,
    w_input,
    w_recur,
    gate_bias,
    w_head,
    remap_dest,
    remap_block,
    remap_weight,
    route_kernel,
    carry_gain,
    block_count,
    parent_section,
    reservoir,
    release,
):
    steps, features, units = forcing.shape
    state = hidden_init.shape[0]
    gates = 4 * state
    reach_blocks, block, _ = route_kernel.shape
    size, unit_size = lax.axis_size("basin"), lax.axis_size("unit")
    rows = reach_blocks * steps
    like = lambda x: pltpu.VMEM(x.shape, x.dtype)
    params = pltpu.CompilerParams(vmem_limit_bytes=(8 << 20) + (size << 18))

    share = pl.pallas_call(
        functools.partial(prep_kernel, size=size),
        out_shape=pltpu.VMEM((PAD, block), jnp.float32),
        in_specs=[HBM] * 3,
        out_specs=VMEM,
        scratch_shapes=[
            pltpu.VMEM((reach_blocks, block), jnp.float32),
            pltpu.VMEM((reach_blocks, block), jnp.float32),
            pltpu.SMEM(block_count.shape, jnp.int32),
            pltpu.SemaphoreType.DMA((3,)),
        ],
        compiler_params=params,
        name="prep",
    )(*in_hbm(block_count, route_kernel, carry_gain))
    shares = share[None]
    order = []
    for bit in gather_bits(size):
        other = lax.ppermute(shares, "basin", [(i, i ^ (1 << bit)) for i in range(size)])
        order.append(other)
        shares = jnp.concatenate([shares, other], axis=0)

    chunk = 256
    parts = 4
    bounds = [0, 1, 6, 11, 12]
    carried = (
        pltpu.VMEM((state, units), jnp.bfloat16),
        pltpu.VMEM((state, units), jnp.float32),
        pltpu.VMEM((PAD, units), jnp.float32),
    )

    def cost(count):
        return pl.CostEstimate(
            flops=2 * count * gates * (state + features) * units,
            bytes_accessed=4 << 20,
            transcendentals=5 * count * state * units,
        )

    forcing_v, table, hidden, cell, head_sum, given = pl.pallas_call(
        functools.partial(first_kernel, count=bounds[1], chunk=chunk),
        out_shape=(
            like(forcing),
            pltpu.VMEM((gates + PAD, 2 * state), jnp.bfloat16),
            *carried,
            pltpu.VMEM((size, block), jnp.float32),
        ),
        in_specs=[HBM] * 8,
        out_specs=(VMEM,) * 6,
        scratch_shapes=[
            pltpu.VMEM((gates, state), jnp.bfloat16),
            pltpu.VMEM((features, gates), jnp.bfloat16),
            pltpu.VMEM((1, gates), jnp.float32),
            pltpu.VMEM((1, state), jnp.float32),
            pltpu.VMEM(release.shape, jnp.float32),
            pltpu.VMEM((block, block), jnp.float32),
            pltpu.SemaphoreType.DMA((steps,)),
            pltpu.SemaphoreType.DMA((7,)),
        ],
        compiler_params=params,
        cost_estimate=cost(bounds[1]),
        name="lstm0",
    )(
        *in_hbm(
            w_recur,
            w_input.T,
            gate_bias.reshape(1, gates),
            w_head.reshape(1, state),
            hidden_init,
            cell_init,
            release,
            forcing,
        )
    )
    for part in range(1, parts):
        last = part == parts - 1
        fetch = {1: (route_kernel, carry_gain), parts - 1: (remap_weight,)}.get(part, ())
        results = (pltpu.VMEM((PAD, units), jnp.bfloat16),) if last else carried
        outs = pl.pallas_call(
            functools.partial(
                later_kernel,
                first=bounds[part],
                count=bounds[part + 1] - bounds[part],
                last=last,
                fetched=len(fetch),
                chunk=chunk,
            ),
            out_shape=results + tuple(like(x) for x in fetch),
            in_specs=[VMEM] * 5 + [pl.BlockSpec(memory_space=pl.ANY)] + [HBM] * len(fetch),
            out_specs=(VMEM,) * (len(results) + len(fetch)),
            scratch_shapes=(list(carried) if last else []) + [pltpu.SemaphoreType.DMA((max(1, len(fetch)),))],
            compiler_params=params,
            cost_estimate=cost(bounds[part + 1] - bounds[part]),
            name=f"lstm{part}",
        )(
            *in_vmem(forcing_v, table, hidden, cell, head_sum),
            order[min(part, len(order)) - 1],
            *in_hbm(*fetch),
        )
        if part == 1:
            route_v, gain_v = outs[len(results) :]
        if last:
            runoff, weight_v = outs
        else:
            hidden, cell, head_sum = outs[:3]
    keep, send, shift = pl.pallas_call(
        functools.partial(remap_kernel, size=size, reach_blocks=reach_blocks, steps=steps),
        out_shape=(
            pltpu.VMEM((size // 2 * rows, block), jnp.bfloat16),
            pltpu.VMEM((size // 2 * rows + 2 * size, block), jnp.bfloat16),
            pltpu.VMEM((size, block), jnp.float32),
        ),
        in_specs=[SMEM, SMEM] + [VMEM] * 3,
        out_specs=(VMEM,) * 3,
        scratch_shapes=[
            pltpu.VMEM((size * reach_blocks, PAD, block), jnp.float32),
            pltpu.VMEM((block, block), jnp.float32),
        ],
        compiler_params=params,
        name="remap",
    )(remap_dest, remap_block, *in_vmem(runoff, weight_v), shares)

    wide = jnp.float32
    exchange = [(at, bit) for at, bit in enumerate(stage_bits(size))]
    across_at = min(1, len(exchange) - 1)
    for at, bit in exchange:
        if at > 0:
            kept = keep.shape[0]
            total = (keep.astype(wide) + got[:kept].astype(wide)).astype(jnp.bfloat16)
            shift = shift + (got[kept : kept + size].astype(wide) + got[kept + size :].astype(wide))
            for part in others:
                shift = shift + part
            keep, send = total[: kept // 2], jnp.concatenate([total[kept // 2 :]] + halves(shift), axis=0)
        swap = 1 << bit
        got = lax.ppermute(send, "basin", [(i, i ^ swap) for i in range(size)])
        others = []
        if at == across_at:
            for turn in range(1, unit_size):
                for hop in (0, swap):
                    route = [
                        (b * unit_size + u, (b ^ hop) * unit_size + (u ^ turn))
                        for b in range(size)
                        for u in range(unit_size)
                    ]
                    others.append(lax.ppermute(shift, AXES, route))
    for part in others:
        shift = shift + part
    return pl.pallas_call(
        functools.partial(finish_kernel, steps=steps, unit_size=unit_size),
        out_shape=jax.ShapeDtypeStruct((steps, reach_blocks * block), jnp.float32),
        in_specs=[SMEM, SMEM, SMEM] + [VMEM] * 6,
        out_specs=VMEM,
        scratch_shapes=[
            pltpu.VMEM((size + 8, block), jnp.float32),
            pltpu.VMEM((unit_size + 1, 2, size, block), jnp.float32),
        ],
        compiler_params=params,
        name="finish",
    )(block_count, parent_section, reservoir, *in_vmem(given), shift, keep, got, *in_vmem(route_v, gain_v))


def solution(mesh):
    placed = (
        P(None, None, AXES),
        P(None, AXES),
        P(None, AXES),
        P(),
        P(),
        P(),
        P(),
        P(AXES, None),
        P(AXES, None),
        P(AXES, None, None, None),
        P(AXES, None, None),
        P(AXES, None),
        P(),
        P(),
        P(),
        P(),
    )
    return jax.shard_map(
        shards, mesh=mesh, in_specs=placed, out_specs=P(None, AXES), check_vma=False
    )
```

```python
import functools

import jax
import jax.numpy as jnp
from jax import lax
from jax.experimental import pallas as pl
from jax.experimental.pallas import tpu as pltpu
from jax.sharding import PartitionSpec as P

PRECISE = lax.Precision.HIGHEST
AXES = ("basin", "unit")
PAD = 16
VMEM = pl.BlockSpec(memory_space=pltpu.VMEM)
SMEM = pl.BlockSpec(memory_space=pltpu.SMEM)
HBM = pl.BlockSpec(memory_space=pltpu.HBM)


def in_hbm(*arrays):
    return [pltpu.with_memory_space_constraint(x, pltpu.HBM) for x in arrays]


def in_vmem(*arrays):
    return [pltpu.with_memory_space_constraint(x, pltpu.VMEM) for x in arrays]


def stage_bits(size):
    return range(size.bit_length() - 1)


def gather_bits(size):
    bits = list(range(size.bit_length() - 1))
    return bits[1:] + bits[:1]


def place_of(relative, size):
    return sum(((relative >> bit) & 1) << at for at, bit in enumerate(gather_bits(size)))


def slot_of(relative, size):
    slot = relative * 0
    for bit in stage_bits(size):
        slot = slot * 2 + ((relative >> bit) & 1)
    return slot


def relative_of(slot, size):
    bits = list(stage_bits(size))
    return sum(((slot >> (len(bits) - 1 - at)) & 1) << bit for at, bit in enumerate(bits))


def split3(x):
    high = x.astype(jnp.bfloat16)
    rest = x - high.astype(jnp.float32)
    middle = rest.astype(jnp.bfloat16)
    low = (rest - middle.astype(jnp.float32)).astype(jnp.bfloat16)
    return high, middle, low


def repeat(count, body):
    if count <= 16:
        for at in range(count):
            body(at)
    else:
        lax.fori_loop(0, count, lambda at, carry: (body(at), carry)[1], 0)


def prep_kernel(count_hbm, route_hbm, gain_hbm, share_ref, last_ref, gain_ref, count_ref, sems, *, size):
    reach_blocks, block = gain_hbm.shape
    copies = [
        pltpu.make_async_copy(route_hbm.at[:, block - 1, :], last_ref, sems.at[0]),
        pltpu.make_async_copy(gain_hbm, gain_ref, sems.at[1]),
        pltpu.make_async_copy(count_hbm, count_ref, sems.at[2]),
    ]
    for copy in copies:
        copy.start()
    for copy in copies:
        copy.wait()
    first = lax.axis_index("unit") * reach_blocks
    count = count_ref[lax.axis_index("basin")]
    factor = jnp.ones((1, block), jnp.float32)
    rows = [None] * reach_blocks
    for blk in reversed(range(reach_blocks)):
        live = first + blk < count
        rows[blk] = jnp.where(live, factor * last_ref[blk : blk + 1, :], 0.0)
        ratio = jnp.broadcast_to(gain_ref[blk : blk + 1, block - 1 : block], (1, block))
        factor = jnp.where(live, factor * ratio, factor)
    rows.append(factor * (1.0 / size))
    rows.append(jnp.zeros((PAD - len(rows), block), jnp.float32))
    share_ref[...] = jnp.concatenate(rows, axis=0)


def advance(table, frame, hidden, cell, hidden_out, cell_out, head_row, *, chunk):
    state, units = hidden.shape
    depth = state + frame.shape[0] + PAD
    ones = jnp.ones((PAD, chunk), jnp.bfloat16)
    for first in range(0, units, chunk):
        cols = pl.ds(first, chunk)
        operand = jnp.concatenate([hidden[:, cols], frame[:, cols], ones], axis=0)

        def gate(at, rows=state):
            piece = table[at * state : at * state + rows, 0:depth]
            return jnp.dot(piece, operand, preferred_element_type=jnp.float32)

        if head_row is not None:
            head = gate(4, PAD)
            head_row[:, cols] = head[0:1] + head[1:2] + head[2:3]
        kept = (jnp.tanh(gate(1)) + 1.0) * cell[:, cols]
        taken = (jnp.tanh(gate(0)) + 1.0) * jnp.tanh(gate(2))
        after = (kept + taken) * 0.5
        cell_out[:, cols] = after
        hidden_out[:, cols] = ((jnp.tanh(gate(3)) + 1.0) * jnp.tanh(after)).astype(jnp.bfloat16)


def build_table(table, w_recur_ref, w_input_ref, bias_ref, head_ref):
    gates, state = w_recur_ref.shape
    features = w_input_ref.shape[0]
    table[gates : gates + PAD, state : 2 * state] = jnp.zeros((PAD, state), jnp.bfloat16)
    for gate in range(4):
        at = pl.ds(gate * state, state)
        scale = 0.5 if gate == 2 else 0.25
        table[at, 0:state] = (w_recur_ref[at, :].astype(jnp.float32) * scale).astype(jnp.bfloat16)
    row = lax.broadcasted_iota(jnp.int32, (state - features, gates), 0)
    bias_rows = jnp.zeros((state - features, gates), jnp.float32)
    for at, part in enumerate(split3(bias_ref[...])):
        part = jnp.broadcast_to(part.astype(jnp.float32), bias_rows.shape)
        bias_rows = jnp.where(row == at, part, bias_rows)
    tail = jnp.concatenate([w_input_ref[...].astype(jnp.float32), bias_rows], axis=0)
    for gate in range(4):
        piece = tail[:, gate * state : (gate + 1) * state] * (1.0 if gate == 2 else 0.5)
        table[gate * state : (gate + 1) * state, state : 2 * state] = piece.T.astype(jnp.bfloat16)
    row = lax.broadcasted_iota(jnp.int32, (PAD, state), 0)
    head_rows = jnp.zeros((PAD, state), jnp.float32)
    for at, part in enumerate(split3(head_ref[...] * 0.5)):
        part = jnp.broadcast_to(part.astype(jnp.float32), head_rows.shape)
        head_rows = jnp.where(row == at, part, head_rows)
    table[gates : gates + PAD, 0:state] = head_rows.astype(jnp.bfloat16)


def first_kernel(
    w_recur_hbm,
    w_input_hbm,
    bias_hbm,
    head_hbm,
    hidden_hbm,
    cell_hbm,
    release_hbm,
    forcing_hbm,
    forcing_ref,
    table,
    hidden,
    cell,
    head_sum,
    given_ref,
    w_recur_ref,
    w_input_ref,
    bias_ref,
    head_ref,
    release_ref,
    square,
    frame_sems,
    sems,
    *,
    count,
    chunk,
):
    steps = forcing_hbm.shape[0]
    pairs = [
        (w_recur_hbm, w_recur_ref),
        (w_input_hbm, w_input_ref),
        (bias_hbm, bias_ref),
        (head_hbm, head_ref),
        (release_hbm, release_ref),
        (hidden_hbm, hidden),
        (cell_hbm, cell),
    ]
    copies = [pltpu.make_async_copy(a, b, sems.at[at]) for at, (a, b) in enumerate(pairs)]
    frames = [
        pltpu.make_async_copy(forcing_hbm.at[now], forcing_ref.at[now], frame_sems.at[now])
        for now in range(steps)
    ]
    for copy in copies + frames:
        copy.start()
    square[...] = jnp.zeros_like(square)
    head_sum[...] = jnp.zeros_like(head_sum)
    for copy in copies[:5]:
        copy.wait()
    build_table(table, w_recur_ref, w_input_ref, bias_ref, head_ref)
    square[0:steps, 0 : release_ref.shape[1]] = release_ref[...]
    given_ref[...] = square[...].T[0 : given_ref.shape[0]]
    for copy in copies[5:]:
        copy.wait()
    hidden[...] = hidden[...] + hidden[...]
    for now in range(count):
        frames[now].wait()
        row = head_sum.at[now - 1 : now] if now > 0 else None
        advance(table, forcing_ref.at[now], hidden, cell, hidden, cell, row, chunk=chunk)
    for now in range(count, steps):
        frames[now].wait()


def later_kernel(*refs, first, count, last, fetched, chunk):
    forcing_ref, table, hidden_in, cell_in, head_in = refs[:5]
    sources, refs = refs[6 : 6 + fetched], refs[6 + fetched :]
    if last:
        runoff_ref, refs = refs[0], refs[1:]
    else:
        (hidden, cell, head_sum), refs = refs[:3], refs[3:]
    targets, refs = refs[:fetched], refs[fetched:]
    if last:
        hidden, cell, head_sum, sems = refs
    else:
        (sems,) = refs
    copies = [pltpu.make_async_copy(a, b, sems.at[at]) for at, (a, b) in enumerate(zip(sources, targets))]
    for copy in copies:
        copy.start()
    state = hidden_in.shape[0]
    gates = 4 * state
    head_sum[...] = head_in[...]
    for now in range(first, first + count):
        begin = now == first
        row = head_sum.at[now - 1 : now]
        old = (hidden_in, cell_in) if begin else (hidden, cell)
        advance(table, forcing_ref.at[now], *old, hidden, cell, row, chunk=chunk)
    if last:
        end = jnp.dot(table[gates : gates + PAD, 0:state], hidden[...], preferred_element_type=jnp.float32)
        now = first + count
        head_sum[now - 1 : now, :] = end[0:1] + end[1:2] + end[2:3]
        runoff_ref[...] = jax.nn.softplus(head_sum[...]).astype(jnp.bfloat16)
    for copy in copies:
        copy.wait()


def remap_kernel(
    dest_ref,
    block_ref,
    runoff_ref,
    weight_ref,
    share_ref,
    keep_ref,
    send_ref,
    shift_ref,
    slots,
    square,
    *,
    size,
    reach_blocks,
    steps,
):
    unit_blocks, fan_out, block, _ = weight_ref.shape
    me = lax.axis_index("basin")
    slots[...] = jnp.zeros_like(slots)
    square[...] = jnp.zeros_like(square)
    for group in range(unit_blocks):
        left = runoff_ref[:, group * block : (group + 1) * block]
        for k in range(0, fan_out, 2):
            right = jnp.concatenate([weight_ref[group, k], weight_ref[group, k + 1]], axis=1)
            both = jnp.dot(left, right, preferred_element_type=jnp.float32)
            for side in range(2):
                slot = slot_of(dest_ref[group, k + side] ^ me, size) * reach_blocks + block_ref[group, k + side]
                slots[slot] = slots[slot] + both[:, side * block : (side + 1) * block]
    half = size // 2
    rows = reach_blocks * steps
    lane = lax.broadcasted_iota(jnp.int32, (PAD, block), 1)
    row = lax.broadcasted_iota(jnp.int32, (PAD, 1), 0)
    origin = lax.axis_index("unit") * PAD

    def gather(at, out_ref, base, columns):
        pieces = [slots[at * reach_blocks + blk] for blk in range(reach_blocks)]
        tile = jnp.concatenate([piece[0:steps] for piece in pieces], axis=0)
        out_ref[pl.ds((at - base) * rows, rows), :] = tile.astype(jnp.bfloat16)
        relative = relative_of(at, size)
        section = relative ^ me
        share = share_ref[place_of(relative, size)]
        total = pieces[0] * share[0:1]
        for blk in range(1, reach_blocks):
            total = total + pieces[blk] * share[blk : blk + 1]
        column = jnp.sum(total, axis=1, keepdims=True)
        column = jnp.where(row == steps, share[reach_blocks : reach_blocks + 1, 0:1], column)
        column = jnp.where(row > steps, 0.0, column)
        return jnp.where(lane == section, column, columns)

    columns = jnp.zeros((PAD, block), jnp.float32)
    if size <= 16:
        for at in range(size):
            columns = gather(at, keep_ref if at < half else send_ref, 0 if at < half else half, columns)
    else:
        columns = lax.fori_loop(0, half, lambda at, c: gather(at, keep_ref, 0, c), columns)
        columns = lax.fori_loop(half, size, lambda at, c: gather(at, send_ref, half, c), columns)
    square[pl.ds(pl.multiple_of(origin, PAD), PAD), :] = columns
    shift = square[...].T[0:size]
    shift_ref[...] = shift
    high = shift.astype(jnp.bfloat16)
    send_ref[half * rows : half * rows + size, :] = high
    send_ref[half * rows + size : half * rows + 2 * size, :] = (shift - high.astype(jnp.float32)).astype(jnp.bfloat16)


def finish_kernel(
    count_ref,
    parent_ref,
    reservoir_ref,
    given_ref,
    shift_ref,
    mine_ref,
    got_ref,
    route_ref,
    gain_ref,
    out_ref,
    inflow,
    joined,
    *,
    steps,
    unit_size,
):
    reach_blocks, block = gain_ref.shape
    size = shift_ref.shape[0]
    basin, unit = lax.axis_index("basin"), lax.axis_index("unit")
    rows = reach_blocks * steps
    high = got_ref[rows : rows + size, :].astype(jnp.float32)
    total = shift_ref[...] + (high + got_ref[rows + size : rows + 2 * size, :].astype(jnp.float32))
    lateral = mine_ref[...].astype(jnp.float32) + got_ref[0:rows, :].astype(jnp.float32)
    flows = []
    for blk in range(reach_blocks):
        flows.append(
            lax.dot_general(
                lateral[blk * steps : (blk + 1) * steps], route_ref[blk], (((1,), (1,)), ((), ())),
                precision=PRECISE, preferred_element_type=jnp.float32,
            )
        )
    shift = jnp.zeros_like(total)
    factor = jnp.ones_like(total)
    for at in range(unit_size):
        own = jnp.broadcast_to(total[:, at * PAD + steps : at * PAD + steps + 1], total.shape)
        moved = total if at == 0 else pltpu.roll(total, block - at * PAD, 1)
        shift = moved + own * shift
        factor = factor * own
        joined[at, 0] = moved
        joined[at, 1] = own
    joined[unit_size, 0] = shift
    joined[unit_size, 1] = factor
    inflow[...] = jnp.zeros_like(inflow)

    def tree(section):
        at = pl.ds(section, 1)
        outflow = joined[unit_size, 0, at, :] + joined[unit_size, 1, at, :] * inflow[at, :]
        passed = jnp.where(reservoir_ref[section] == 1, given_ref[at, :], outflow)
        parent = pl.ds(parent_ref[section], 1)
        inflow[parent, :] = inflow[parent, :] + passed

    repeat(size, tree)
    here = pl.ds(basin, 1)
    head = inflow[here, :]
    for at in range(unit_size - 1):
        head = jnp.where(at < unit, joined[at, 0, here, :] + joined[at, 1, here, :] * head, head)
    lane = lax.broadcasted_iota(jnp.int32, (PAD, block), 1)
    row = lax.broadcasted_iota(jnp.int32, (PAD, block), 0)
    column = jnp.sum(jnp.where(lane == row, jnp.broadcast_to(head, lane.shape), 0.0), axis=1, keepdims=True)
    carry = jnp.broadcast_to(column[0:steps], (steps, block))
    count = count_ref[basin]
    for blk in range(reach_blocks):
        live = unit * reach_blocks + blk < count
        flow = flows[blk] + carry * gain_ref[blk : blk + 1, :]
        out_ref[:, blk * block : (blk + 1) * block] = jnp.where(live, flow, 0.0)
        carry = jnp.where(live, jnp.broadcast_to(flow[:, block - 1 : block], carry.shape), carry)


def halves(shift):
    high = lax.reduce_precision(shift, 8, 7)
    return [high.astype(jnp.bfloat16), lax.reduce_precision(shift - high, 8, 7).astype(jnp.bfloat16)]


def shards(
    forcing,
    hidden_init,
    cell_init,
    w_input,
    w_recur,
    gate_bias,
    w_head,
    remap_dest,
    remap_block,
    remap_weight,
    route_kernel,
    carry_gain,
    block_count,
    parent_section,
    reservoir,
    release,
):
    steps, features, units = forcing.shape
    state = hidden_init.shape[0]
    gates = 4 * state
    reach_blocks, block, _ = route_kernel.shape
    size, unit_size = lax.axis_size("basin"), lax.axis_size("unit")
    rows = reach_blocks * steps
    like = lambda x: pltpu.VMEM(x.shape, x.dtype)
    params = pltpu.CompilerParams(vmem_limit_bytes=(8 << 20) + (size << 18))

    share = pl.pallas_call(
        functools.partial(prep_kernel, size=size),
        out_shape=pltpu.VMEM((PAD, block), jnp.float32),
        in_specs=[HBM] * 3,
        out_specs=VMEM,
        scratch_shapes=[
            pltpu.VMEM((reach_blocks, block), jnp.float32),
            pltpu.VMEM((reach_blocks, block), jnp.float32),
            pltpu.SMEM(block_count.shape, jnp.int32),
            pltpu.SemaphoreType.DMA((3,)),
        ],
        compiler_params=params,
        name="prep",
    )(*in_hbm(block_count, route_kernel, carry_gain))
    shares = share[None]
    order = []
    for bit in gather_bits(size):
        other = lax.ppermute(shares, "basin", [(i, i ^ (1 << bit)) for i in range(size)])
        order.append(other)
        shares = jnp.concatenate([shares, other], axis=0)

    chunk = 256
    parts = 3
    bounds = [0, 1, steps // 2, steps]
    carried = (
        pltpu.VMEM((state, units), jnp.bfloat16),
        pltpu.VMEM((state, units), jnp.float32),
        pltpu.VMEM((PAD, units), jnp.float32),
    )

    def cost(count):
        return pl.CostEstimate(
            flops=2 * count * gates * (state + features) * units,
            bytes_accessed=4 << 20,
            transcendentals=5 * count * state * units,
        )

    forcing_v, table, hidden, cell, head_sum, given = pl.pallas_call(
        functools.partial(first_kernel, count=bounds[1], chunk=chunk),
        out_shape=(
            like(forcing),
            pltpu.VMEM((gates + PAD, 2 * state), jnp.bfloat16),
            *carried,
            pltpu.VMEM((size, block), jnp.float32),
        ),
        in_specs=[HBM] * 8,
        out_specs=(VMEM,) * 6,
        scratch_shapes=[
            pltpu.VMEM((gates, state), jnp.bfloat16),
            pltpu.VMEM((features, gates), jnp.bfloat16),
            pltpu.VMEM((1, gates), jnp.float32),
            pltpu.VMEM((1, state), jnp.float32),
            pltpu.VMEM(release.shape, jnp.float32),
            pltpu.VMEM((block, block), jnp.float32),
            pltpu.SemaphoreType.DMA((steps,)),
            pltpu.SemaphoreType.DMA((7,)),
        ],
        compiler_params=params,
        cost_estimate=cost(bounds[1]),
        name="lstm0",
    )(
        *in_hbm(
            w_recur,
            w_input.T,
            gate_bias.reshape(1, gates),
            w_head.reshape(1, state),
            hidden_init,
            cell_init,
            release,
            forcing,
        )
    )
    for part in range(1, parts):
        last = part == parts - 1
        fetch = {1: (route_kernel, carry_gain), parts - 1: (remap_weight,)}.get(part, ())
        results = (pltpu.VMEM((PAD, units), jnp.bfloat16),) if last else carried
        outs = pl.pallas_call(
            functools.partial(
                later_kernel,
                first=bounds[part],
                count=bounds[part + 1] - bounds[part],
                last=last,
                fetched=len(fetch),
                chunk=chunk,
            ),
            out_shape=results + tuple(like(x) for x in fetch),
            in_specs=[VMEM] * 5 + [pl.BlockSpec(memory_space=pl.ANY)] + [HBM] * len(fetch),
            out_specs=(VMEM,) * (len(results) + len(fetch)),
            scratch_shapes=(list(carried) if last else []) + [pltpu.SemaphoreType.DMA((max(1, len(fetch)),))],
            compiler_params=params,
            cost_estimate=cost(bounds[part + 1] - bounds[part]),
            name=f"lstm{part}",
        )(
            *in_vmem(forcing_v, table, hidden, cell, head_sum),
            order[min(part, len(order)) - 1],
            *in_hbm(*fetch),
        )
        if part == 1:
            route_v, gain_v = outs[len(results) :]
        if last:
            runoff, weight_v = outs
        else:
            hidden, cell, head_sum = outs[:3]
    keep, send, shift = pl.pallas_call(
        functools.partial(remap_kernel, size=size, reach_blocks=reach_blocks, steps=steps),
        out_shape=(
            pltpu.VMEM((size // 2 * rows, block), jnp.bfloat16),
            pltpu.VMEM((size // 2 * rows + 2 * size, block), jnp.bfloat16),
            pltpu.VMEM((size, block), jnp.float32),
        ),
        in_specs=[SMEM, SMEM] + [VMEM] * 3,
        out_specs=(VMEM,) * 3,
        scratch_shapes=[
            pltpu.VMEM((size * reach_blocks, PAD, block), jnp.float32),
            pltpu.VMEM((block, block), jnp.float32),
        ],
        compiler_params=params,
        name="remap",
    )(remap_dest, remap_block, *in_vmem(runoff, weight_v), shares)

    wide = jnp.float32
    exchange = [(at, bit) for at, bit in enumerate(stage_bits(size))]
    across_at = min(1, len(exchange) - 1)
    for at, bit in exchange:
        if at > 0:
            kept = keep.shape[0]
            total = (keep.astype(wide) + got[:kept].astype(wide)).astype(jnp.bfloat16)
            shift = shift + (got[kept : kept + size].astype(wide) + got[kept + size :].astype(wide))
            for part in others:
                shift = shift + part
            keep, send = total[: kept // 2], jnp.concatenate([total[kept // 2 :]] + halves(shift), axis=0)
        swap = 1 << bit
        got = lax.ppermute(send, "basin", [(i, i ^ swap) for i in range(size)])
        others = []
        if at == across_at:
            for turn in range(1, unit_size):
                for hop in (0, swap):
                    route = [
                        (b * unit_size + u, (b ^ hop) * unit_size + (u ^ turn))
                        for b in range(size)
                        for u in range(unit_size)
                    ]
                    others.append(lax.ppermute(shift, AXES, route))
    for part in others:
        shift = shift + part
    return pl.pallas_call(
        functools.partial(finish_kernel, steps=steps, unit_size=unit_size),
        out_shape=jax.ShapeDtypeStruct((steps, reach_blocks * block), jnp.float32),
        in_specs=[SMEM, SMEM, SMEM] + [VMEM] * 6,
        out_specs=VMEM,
        scratch_shapes=[
            pltpu.VMEM((size + 8, block), jnp.float32),
            pltpu.VMEM((unit_size + 1, 2, size, block), jnp.float32),
        ],
        compiler_params=params,
        name="finish",
    )(block_count, parent_section, reservoir, *in_vmem(given), shift, keep, got, *in_vmem(route_v, gain_v))


def solution(mesh):
    placed = (
        P(None, None, AXES),
        P(None, AXES),
        P(None, AXES),
        P(),
        P(),
        P(),
        P(),
        P(AXES, None),
        P(AXES, None),
        P(AXES, None, None, None),
        P(AXES, None, None),
        P(AXES, None),
        P(),
        P(),
        P(),
        P(),
    )
    return jax.shard_map(
        shards, mesh=mesh, in_specs=placed, out_specs=P(None, AXES), check_vma=False
    )
```

```python
import functools

import jax
import jax.numpy as jnp
from jax import lax
from jax.experimental import pallas as pl
from jax.experimental.pallas import tpu as pltpu
from jax.sharding import PartitionSpec as P

PRECISE = lax.Precision.HIGHEST
AXES = ("basin", "unit")
PAD = 16
VMEM = pl.BlockSpec(memory_space=pltpu.VMEM)
SMEM = pl.BlockSpec(memory_space=pltpu.SMEM)
HBM = pl.BlockSpec(memory_space=pltpu.HBM)


def in_hbm(*arrays):
    return [pltpu.with_memory_space_constraint(x, pltpu.HBM) for x in arrays]


def in_vmem(*arrays):
    return [pltpu.with_memory_space_constraint(x, pltpu.VMEM) for x in arrays]


def stage_bits(size):
    return range(size.bit_length() - 1)


def gather_bits(size):
    bits = list(range(size.bit_length() - 1))
    return bits[1:] + bits[:1]


def place_of(relative, size):
    return sum(((relative >> bit) & 1) << at for at, bit in enumerate(gather_bits(size)))


def slot_of(relative, size):
    slot = relative * 0
    for bit in stage_bits(size):
        slot = slot * 2 + ((relative >> bit) & 1)
    return slot


def relative_of(slot, size):
    bits = list(stage_bits(size))
    return sum(((slot >> (len(bits) - 1 - at)) & 1) << bit for at, bit in enumerate(bits))


def split3(x):
    high = x.astype(jnp.bfloat16)
    rest = x - high.astype(jnp.float32)
    middle = rest.astype(jnp.bfloat16)
    low = (rest - middle.astype(jnp.float32)).astype(jnp.bfloat16)
    return high, middle, low


def repeat(count, body):
    if count <= 16:
        for at in range(count):
            body(at)
    else:
        lax.fori_loop(0, count, lambda at, carry: (body(at), carry)[1], 0)


def prep_kernel(count_hbm, route_hbm, gain_hbm, share_ref, last_ref, gain_ref, count_ref, sems, *, size):
    reach_blocks, block = gain_hbm.shape
    copies = [
        pltpu.make_async_copy(route_hbm.at[:, block - 1, :], last_ref, sems.at[0]),
        pltpu.make_async_copy(gain_hbm, gain_ref, sems.at[1]),
        pltpu.make_async_copy(count_hbm, count_ref, sems.at[2]),
    ]
    for copy in copies:
        copy.start()
    for copy in copies:
        copy.wait()
    first = lax.axis_index("unit") * reach_blocks
    count = count_ref[lax.axis_index("basin")]
    factor = jnp.ones((1, block), jnp.float32)
    rows = [None] * reach_blocks
    for blk in reversed(range(reach_blocks)):
        live = first + blk < count
        rows[blk] = jnp.where(live, factor * last_ref[blk : blk + 1, :], 0.0)
        ratio = jnp.broadcast_to(gain_ref[blk : blk + 1, block - 1 : block], (1, block))
        factor = jnp.where(live, factor * ratio, factor)
    rows.append(factor * (1.0 / size))
    rows.append(jnp.zeros((PAD - len(rows), block), jnp.float32))
    share_ref[...] = jnp.concatenate(rows, axis=0)


def advance(table, frame, hidden, cell, hidden_out, cell_out, head_row, *, chunk):
    state, units = hidden.shape
    depth = state + frame.shape[0] + PAD
    ones = jnp.ones((PAD, chunk), jnp.bfloat16)
    for first in range(0, units, chunk):
        cols = pl.ds(first, chunk)
        operand = jnp.concatenate([hidden[:, cols], frame[:, cols], ones], axis=0)

        def gate(at, rows=state):
            piece = table[at * state : at * state + rows, 0:depth]
            return jnp.dot(piece, operand, preferred_element_type=jnp.float32)

        if head_row is not None:
            head = gate(4, PAD)
            head_row[:, cols] = head[0:1] + head[1:2] + head[2:3]
        kept = (jnp.tanh(gate(1)) + 1.0) * cell[:, cols]
        taken = (jnp.tanh(gate(0)) + 1.0) * jnp.tanh(gate(2))
        after = (kept + taken) * 0.5
        cell_out[:, cols] = after
        hidden_out[:, cols] = ((jnp.tanh(gate(3)) + 1.0) * jnp.tanh(after)).astype(jnp.bfloat16)


def build_table(table, w_recur_ref, w_input_ref, bias_ref, head_ref):
    gates, state = w_recur_ref.shape
    features = w_input_ref.shape[0]
    table[gates : gates + PAD, state : 2 * state] = jnp.zeros((PAD, state), jnp.bfloat16)
    for gate in range(4):
        at = pl.ds(gate * state, state)
        scale = 0.5 if gate == 2 else 0.25
        table[at, 0:state] = (w_recur_ref[at, :].astype(jnp.float32) * scale).astype(jnp.bfloat16)
    row = lax.broadcasted_iota(jnp.int32, (state - features, gates), 0)
    bias_rows = jnp.zeros((state - features, gates), jnp.float32)
    for at, part in enumerate(split3(bias_ref[...])):
        part = jnp.broadcast_to(part.astype(jnp.float32), bias_rows.shape)
        bias_rows = jnp.where(row == at, part, bias_rows)
    tail = jnp.concatenate([w_input_ref[...].astype(jnp.float32), bias_rows], axis=0)
    for gate in range(4):
        piece = tail[:, gate * state : (gate + 1) * state] * (1.0 if gate == 2 else 0.5)
        table[gate * state : (gate + 1) * state, state : 2 * state] = piece.T.astype(jnp.bfloat16)
    row = lax.broadcasted_iota(jnp.int32, (PAD, state), 0)
    head_rows = jnp.zeros((PAD, state), jnp.float32)
    for at, part in enumerate(split3(head_ref[...] * 0.5)):
        part = jnp.broadcast_to(part.astype(jnp.float32), head_rows.shape)
        head_rows = jnp.where(row == at, part, head_rows)
    table[gates : gates + PAD, 0:state] = head_rows.astype(jnp.bfloat16)


def first_kernel(
    w_recur_hbm,
    w_input_hbm,
    bias_hbm,
    head_hbm,
    hidden_hbm,
    cell_hbm,
    release_hbm,
    forcing_hbm,
    forcing_ref,
    table,
    hidden,
    cell,
    head_sum,
    given_ref,
    w_recur_ref,
    w_input_ref,
    bias_ref,
    head_ref,
    release_ref,
    square,
    frame_sems,
    sems,
    *,
    count,
    chunk,
):
    steps = forcing_hbm.shape[0]
    pairs = [
        (w_recur_hbm, w_recur_ref),
        (w_input_hbm, w_input_ref),
        (bias_hbm, bias_ref),
        (head_hbm, head_ref),
        (release_hbm, release_ref),
        (hidden_hbm, hidden),
        (cell_hbm, cell),
    ]
    copies = [pltpu.make_async_copy(a, b, sems.at[at]) for at, (a, b) in enumerate(pairs)]
    frames = [
        pltpu.make_async_copy(forcing_hbm.at[now], forcing_ref.at[now], frame_sems.at[now])
        for now in range(steps)
    ]
    for copy in copies + frames:
        copy.start()
    square[...] = jnp.zeros_like(square)
    head_sum[...] = jnp.zeros_like(head_sum)
    for copy in copies[:5]:
        copy.wait()
    build_table(table, w_recur_ref, w_input_ref, bias_ref, head_ref)
    square[0:steps, 0 : release_ref.shape[1]] = release_ref[...]
    given_ref[...] = square[...].T[0 : given_ref.shape[0]]
    for copy in copies[5:]:
        copy.wait()
    hidden[...] = hidden[...] + hidden[...]
    for now in range(count):
        frames[now].wait()
        row = head_sum.at[now - 1 : now] if now > 0 else None
        advance(table, forcing_ref.at[now], hidden, cell, hidden, cell, row, chunk=chunk)
    for now in range(count, steps):
        frames[now].wait()


def later_kernel(*refs, first, count, last, fetched, chunk):
    forcing_ref, table, hidden_in, cell_in, head_in = refs[:5]
    sources, refs = refs[6 : 6 + fetched], refs[6 + fetched :]
    if last:
        runoff_ref, refs = refs[0], refs[1:]
    else:
        (hidden, cell, head_sum), refs = refs[:3], refs[3:]
    targets, refs = refs[:fetched], refs[fetched:]
    if last:
        hidden, cell, head_sum, sems = refs
    else:
        (sems,) = refs
    copies = [pltpu.make_async_copy(a, b, sems.at[at]) for at, (a, b) in enumerate(zip(sources, targets))]
    for copy in copies:
        copy.start()
    state = hidden_in.shape[0]
    gates = 4 * state
    head_sum[...] = head_in[...]
    for now in range(first, first + count):
        begin = now == first
        row = head_sum.at[now - 1 : now]
        old = (hidden_in, cell_in) if begin else (hidden, cell)
        advance(table, forcing_ref.at[now], *old, hidden, cell, row, chunk=chunk)
    if last:
        end = jnp.dot(table[gates : gates + PAD, 0:state], hidden[...], preferred_element_type=jnp.float32)
        now = first + count
        head_sum[now - 1 : now, :] = end[0:1] + end[1:2] + end[2:3]
        runoff_ref[...] = jax.nn.softplus(head_sum[...]).astype(jnp.bfloat16)
    for copy in copies:
        copy.wait()


def remap_kernel(
    dest_ref,
    block_ref,
    runoff_ref,
    weight_ref,
    share_ref,
    keep_ref,
    send_ref,
    shift_ref,
    slots,
    square,
    *,
    size,
    reach_blocks,
    steps,
):
    unit_blocks, fan_out, block, _ = weight_ref.shape
    me = lax.axis_index("basin")
    slots[...] = jnp.zeros_like(slots)
    square[...] = jnp.zeros_like(square)
    for group in range(unit_blocks):
        left = runoff_ref[:, group * block : (group + 1) * block]
        for k in range(0, fan_out, 2):
            right = jnp.concatenate([weight_ref[group, k], weight_ref[group, k + 1]], axis=1)
            both = jnp.dot(left, right, preferred_element_type=jnp.float32)
            for side in range(2):
                slot = slot_of(dest_ref[group, k + side] ^ me, size) * reach_blocks + block_ref[group, k + side]
                slots[slot] = slots[slot] + both[:, side * block : (side + 1) * block]
    half = size // 2
    rows = reach_blocks * steps
    lane = lax.broadcasted_iota(jnp.int32, (PAD, block), 1)
    row = lax.broadcasted_iota(jnp.int32, (PAD, 1), 0)
    origin = lax.axis_index("unit") * PAD

    def gather(at, out_ref, base, columns):
        pieces = [slots[at * reach_blocks + blk] for blk in range(reach_blocks)]
        tile = jnp.concatenate([piece[0:steps] for piece in pieces], axis=0)
        out_ref[pl.ds((at - base) * rows, rows), :] = tile.astype(jnp.bfloat16)
        relative = relative_of(at, size)
        section = relative ^ me
        share = share_ref[place_of(relative, size)]
        total = pieces[0] * share[0:1]
        for blk in range(1, reach_blocks):
            total = total + pieces[blk] * share[blk : blk + 1]
        column = jnp.sum(total, axis=1, keepdims=True)
        column = jnp.where(row == steps, share[reach_blocks : reach_blocks + 1, 0:1], column)
        column = jnp.where(row > steps, 0.0, column)
        return jnp.where(lane == section, column, columns)

    columns = jnp.zeros((PAD, block), jnp.float32)
    if size <= 16:
        for at in range(size):
            columns = gather(at, keep_ref if at < half else send_ref, 0 if at < half else half, columns)
    else:
        columns = lax.fori_loop(0, half, lambda at, c: gather(at, keep_ref, 0, c), columns)
        columns = lax.fori_loop(half, size, lambda at, c: gather(at, send_ref, half, c), columns)
    square[pl.ds(pl.multiple_of(origin, PAD), PAD), :] = columns
    shift = square[...].T[0:size]
    shift_ref[...] = shift
    high = shift.astype(jnp.bfloat16)
    send_ref[half * rows : half * rows + size, :] = high
    send_ref[half * rows + size : half * rows + 2 * size, :] = (shift - high.astype(jnp.float32)).astype(jnp.bfloat16)


def finish_kernel(
    count_ref,
    parent_ref,
    reservoir_ref,
    given_ref,
    shift_ref,
    mine_ref,
    got_ref,
    route_ref,
    gain_ref,
    out_ref,
    inflow,
    joined,
    *,
    steps,
    unit_size,
):
    reach_blocks, block = gain_ref.shape
    size = shift_ref.shape[0]
    basin, unit = lax.axis_index("basin"), lax.axis_index("unit")
    rows = reach_blocks * steps
    high = got_ref[rows : rows + size, :].astype(jnp.float32)
    total = shift_ref[...] + (high + got_ref[rows + size : rows + 2 * size, :].astype(jnp.float32))
    lateral = mine_ref[...].astype(jnp.float32) + got_ref[0:rows, :].astype(jnp.float32)
    flows = []
    for blk in range(reach_blocks):
        flows.append(
            lax.dot_general(
                lateral[blk * steps : (blk + 1) * steps], route_ref[blk], (((1,), (1,)), ((), ())),
                precision=PRECISE, preferred_element_type=jnp.float32,
            )
        )
    shift = jnp.zeros_like(total)
    factor = jnp.ones_like(total)
    for at in range(unit_size):
        own = jnp.broadcast_to(total[:, at * PAD + steps : at * PAD + steps + 1], total.shape)
        moved = total if at == 0 else pltpu.roll(total, block - at * PAD, 1)
        shift = moved + own * shift
        factor = factor * own
        joined[at, 0] = moved
        joined[at, 1] = own
    joined[unit_size, 0] = shift
    joined[unit_size, 1] = factor
    inflow[...] = jnp.zeros_like(inflow)

    def tree(section):
        at = pl.ds(section, 1)
        outflow = joined[unit_size, 0, at, :] + joined[unit_size, 1, at, :] * inflow[at, :]
        passed = jnp.where(reservoir_ref[section] == 1, given_ref[at, :], outflow)
        parent = pl.ds(parent_ref[section], 1)
        inflow[parent, :] = inflow[parent, :] + passed

    repeat(size, tree)
    here = pl.ds(basin, 1)
    head = inflow[here, :]
    for at in range(unit_size - 1):
        head = jnp.where(at < unit, joined[at, 0, here, :] + joined[at, 1, here, :] * head, head)
    lane = lax.broadcasted_iota(jnp.int32, (PAD, block), 1)
    row = lax.broadcasted_iota(jnp.int32, (PAD, block), 0)
    column = jnp.sum(jnp.where(lane == row, jnp.broadcast_to(head, lane.shape), 0.0), axis=1, keepdims=True)
    carry = jnp.broadcast_to(column[0:steps], (steps, block))
    count = count_ref[basin]
    for blk in range(reach_blocks):
        live = unit * reach_blocks + blk < count
        flow = flows[blk] + carry * gain_ref[blk : blk + 1, :]
        out_ref[:, blk * block : (blk + 1) * block] = jnp.where(live, flow, 0.0)
        carry = jnp.where(live, jnp.broadcast_to(flow[:, block - 1 : block], carry.shape), carry)


def halves(shift):
    high = lax.reduce_precision(shift, 8, 7)
    return [high.astype(jnp.bfloat16), lax.reduce_precision(shift - high, 8, 7).astype(jnp.bfloat16)]


def shards(
    forcing,
    hidden_init,
    cell_init,
    w_input,
    w_recur,
    gate_bias,
    w_head,
    remap_dest,
    remap_block,
    remap_weight,
    route_kernel,
    carry_gain,
    block_count,
    parent_section,
    reservoir,
    release,
):
    steps, features, units = forcing.shape
    state = hidden_init.shape[0]
    gates = 4 * state
    reach_blocks, block, _ = route_kernel.shape
    size, unit_size = lax.axis_size("basin"), lax.axis_size("unit")
    rows = reach_blocks * steps
    like = lambda x: pltpu.VMEM(x.shape, x.dtype)
    params = pltpu.CompilerParams(vmem_limit_bytes=(8 << 20) + (size << 18))

    share = pl.pallas_call(
        functools.partial(prep_kernel, size=size),
        out_shape=pltpu.VMEM((PAD, block), jnp.float32),
        in_specs=[HBM] * 3,
        out_specs=VMEM,
        scratch_shapes=[
            pltpu.VMEM((reach_blocks, block), jnp.float32),
            pltpu.VMEM((reach_blocks, block), jnp.float32),
            pltpu.SMEM(block_count.shape, jnp.int32),
            pltpu.SemaphoreType.DMA((3,)),
        ],
        compiler_params=params,
        name="prep",
    )(*in_hbm(block_count, route_kernel, carry_gain))
    shares = share[None]
    order = []
    for bit in gather_bits(size):
        other = lax.ppermute(shares, "basin", [(i, i ^ (1 << bit)) for i in range(size)])
        order.append(other)
        shares = jnp.concatenate([shares, other], axis=0)

    chunk = 256
    parts = 3
    bounds = [0, 1, steps * 5 // 12, steps]
    carried = (
        pltpu.VMEM((state, units), jnp.bfloat16),
        pltpu.VMEM((state, units), jnp.float32),
        pltpu.VMEM((PAD, units), jnp.float32),
    )

    def cost(count):
        return pl.CostEstimate(
            flops=2 * count * gates * (state + features) * units,
            bytes_accessed=4 << 20,
            transcendentals=5 * count * state * units,
        )

    forcing_v, table, hidden, cell, head_sum, given = pl.pallas_call(
        functools.partial(first_kernel, count=bounds[1], chunk=chunk),
        out_shape=(
            like(forcing),
            pltpu.VMEM((gates + PAD, 2 * state), jnp.bfloat16),
            *carried,
            pltpu.VMEM((size, block), jnp.float32),
        ),
        in_specs=[HBM] * 8,
        out_specs=(VMEM,) * 6,
        scratch_shapes=[
            pltpu.VMEM((gates, state), jnp.bfloat16),
            pltpu.VMEM((features, gates), jnp.bfloat16),
            pltpu.VMEM((1, gates), jnp.float32),
            pltpu.VMEM((1, state), jnp.float32),
            pltpu.VMEM(release.shape, jnp.float32),
            pltpu.VMEM((block, block), jnp.float32),
            pltpu.SemaphoreType.DMA((steps,)),
            pltpu.SemaphoreType.DMA((7,)),
        ],
        compiler_params=params,
        cost_estimate=cost(bounds[1]),
        name="lstm0",
    )(
        *in_hbm(
            w_recur,
            w_input.T,
            gate_bias.reshape(1, gates),
            w_head.reshape(1, state),
            hidden_init,
            cell_init,
            release,
            forcing,
        )
    )
    for part in range(1, parts):
        last = part == parts - 1
        fetch = {1: (route_kernel, carry_gain), parts - 1: (remap_weight,)}.get(part, ())
        results = (pltpu.VMEM((PAD, units), jnp.bfloat16),) if last else carried
        outs = pl.pallas_call(
            functools.partial(
                later_kernel,
                first=bounds[part],
                count=bounds[part + 1] - bounds[part],
                last=last,
                fetched=len(fetch),
                chunk=chunk,
            ),
            out_shape=results + tuple(like(x) for x in fetch),
            in_specs=[VMEM] * 5 + [pl.BlockSpec(memory_space=pl.ANY)] + [HBM] * len(fetch),
            out_specs=(VMEM,) * (len(results) + len(fetch)),
            scratch_shapes=(list(carried) if last else []) + [pltpu.SemaphoreType.DMA((max(1, len(fetch)),))],
            compiler_params=params,
            cost_estimate=cost(bounds[part + 1] - bounds[part]),
            name=f"lstm{part}",
        )(
            *in_vmem(forcing_v, table, hidden, cell, head_sum),
            order[min(part, len(order)) - 1],
            *in_hbm(*fetch),
        )
        if part == 1:
            route_v, gain_v = outs[len(results) :]
        if last:
            runoff, weight_v = outs
        else:
            hidden, cell, head_sum = outs[:3]
    keep, send, shift = pl.pallas_call(
        functools.partial(remap_kernel, size=size, reach_blocks=reach_blocks, steps=steps),
        out_shape=(
            pltpu.VMEM((size // 2 * rows, block), jnp.bfloat16),
            pltpu.VMEM((size // 2 * rows + 2 * size, block), jnp.bfloat16),
            pltpu.VMEM((size, block), jnp.float32),
        ),
        in_specs=[SMEM, SMEM] + [VMEM] * 3,
        out_specs=(VMEM,) * 3,
        scratch_shapes=[
            pltpu.VMEM((size * reach_blocks, PAD, block), jnp.float32),
            pltpu.VMEM((block, block), jnp.float32),
        ],
        compiler_params=params,
        name="remap",
    )(remap_dest, remap_block, *in_vmem(runoff, weight_v), shares)

    wide = jnp.float32
    exchange = [(at, bit) for at, bit in enumerate(stage_bits(size))]
    across_at = min(1, len(exchange) - 1)
    for at, bit in exchange:
        if at > 0:
            kept = keep.shape[0]
            total = (keep.astype(wide) + got[:kept].astype(wide)).astype(jnp.bfloat16)
            shift = shift + (got[kept : kept + size].astype(wide) + got[kept + size :].astype(wide))
            for part in others:
                shift = shift + part
            keep, send = total[: kept // 2], jnp.concatenate([total[kept // 2 :]] + halves(shift), axis=0)
        swap = 1 << bit
        got = lax.ppermute(send, "basin", [(i, i ^ swap) for i in range(size)])
        others = []
        if at == across_at:
            for turn in range(1, unit_size):
                for hop in (0, swap):
                    route = [
                        (b * unit_size + u, (b ^ hop) * unit_size + (u ^ turn))
                        for b in range(size)
                        for u in range(unit_size)
                    ]
                    others.append(lax.ppermute(shift, AXES, route))
    for part in others:
        shift = shift + part
    return pl.pallas_call(
        functools.partial(finish_kernel, steps=steps, unit_size=unit_size),
        out_shape=jax.ShapeDtypeStruct((steps, reach_blocks * block), jnp.float32),
        in_specs=[SMEM, SMEM, SMEM] + [VMEM] * 6,
        out_specs=VMEM,
        scratch_shapes=[
            pltpu.VMEM((size + 8, block), jnp.float32),
            pltpu.VMEM((unit_size + 1, 2, size, block), jnp.float32),
        ],
        compiler_params=params,
        name="finish",
    )(block_count, parent_section, reservoir, *in_vmem(given), shift, keep, got, *in_vmem(route_v, gain_v))


def solution(mesh):
    placed = (
        P(None, None, AXES),
        P(None, AXES),
        P(None, AXES),
        P(),
        P(),
        P(),
        P(),
        P(AXES, None),
        P(AXES, None),
        P(AXES, None, None, None),
        P(AXES, None, None),
        P(AXES, None),
        P(),
        P(),
        P(),
        P(),
    )
    return jax.shard_map(
        shards, mesh=mesh, in_specs=placed, out_specs=P(None, AXES), check_vma=False
    )
```
